512 devices in a mesh: slab: 128 (over y, z, core), led: 4 (over x).
Axes of the slice: x: 4, y: 4, z: 16, core: 2. Of those that a mesh axis runs over, the one named last changes fastest.
Arguments:
- spectrum: float32 [2, 2048, 2048], P(None, 'slab'), may hold values from -6 to 6
- led_rows: int32 [8], P('led'), may hold values from 256 to 768
- led_cols: int32 [8], P('led'), may hold values from 0 to 1024
- images: float32 [8, 1024, 1024], P('led', 'slab'), may hold values from 0.05 to 4
Outputs:
- updated: float32 [2, 2048, 2048], P(None, 'slab', 'led')
The draws below stay inside these ranges and needn't reach their ends.
All inputs are finite; a program needn't handle non-finite values.
Results may differ from the reference program's by a relative error of at most 0.0065.
Values may be sent and summed in bfloat16 or wider, within the bound.
A program may use at most 64 MiB of HBM per device.

```python
import math
import jax
import jax.numpy as jnp
from jax import lax

WIN = 1024
NROW = 2048
NCOL = 2048
LEDS = 8


def plant(values, stream_key, low, high):
    longest = values.shape.index(max(values.shape))
    spots = []
    for shift in (0, 1):
        where = [jax.random.randint(jax.random.fold_in(stream_key, axis), (), 0, length) for axis, length in enumerate(values.shape)]
        where[longest] = (where[longest] + shift) % values.shape[longest]
        spots.append(tuple(where))
    return values.at[spots[0]].set(low).at[spots[1]].set(high)


def levels(stream_key, shape, split, low, top_value):
    loudness = 1.0
    for axis_at, shards_of in split:
        steps = jax.random.uniform(jax.random.fold_in(jax.random.fold_in(stream_key, 6), axis_at), (shards_of,), jnp.float32, low / len(split), top_value / len(split))
        loudness = loudness * jnp.repeat(jnp.exp(steps), shape[axis_at] // shards_of).reshape((-1,) + (1,) * (len(shape) - 1 - axis_at))
    return loudness


def noise(stream_key, extent, scale, most, pieces=(), held_as=jnp.bfloat16):
    result = scale * jax.random.normal(stream_key, extent, jnp.float32)
    if pieces:
        result = result * levels(stream_key, extent, pieces, -0.22, 0.18)
    return jnp.clip(result, -most, most).astype(held_as)


def setup_inputs(seed: int = 0) -> dict:
    keys = jax.random.split(jax.random.key(seed), 5)
    spectrum = noise(keys[0], (2, NROW, NCOL), 1.0, 6.0, ((1, 128),), jnp.float32)
    led_rows = plant(jax.random.randint(keys[1], (LEDS,), (NROW - WIN) // 4, 3 * (NROW - WIN) // 4 + 1), jax.random.fold_in(keys[1], 1), (NROW - WIN) // 4, (3 * (NROW - WIN) // 4 + 1) - 1).astype(jnp.int32)
    led_cols = plant(jax.random.randint(keys[2], (LEDS,), 0, NCOL - WIN + 1), jax.random.fold_in(keys[2], 1), 0, NCOL - WIN).astype(jnp.int32)
    images = jnp.clip(jnp.exp(math.log(4.0) - 4.3820266 * jax.random.uniform(keys[3], (LEDS, WIN, WIN), jnp.float32) ** levels(keys[3], (LEDS, WIN, WIN), ((0, 4), (1, 128)), -0.2, 0.2)), 0.05, 4.0)
    return dict(spectrum=spectrum, led_rows=led_rows, led_cols=led_cols, images=images)


def make_tables(width):
    index = jnp.arange(width, dtype=jnp.int32)
    angle_index = index[:, None] * index[None, :] % width
    angle = angle_index.astype(jnp.float32) * (2.0 * 3.141592653589793 / width)
    scale = 1.0 / jnp.sqrt(jnp.float32(width))
    return ((jnp.cos(angle) * scale).astype(jnp.bfloat16), (jnp.sin(angle) * scale).astype(jnp.bfloat16))

def make_pupil(row_index, col_index, width):
    row_term = (2 * row_index + 1 - width) * (2 * row_index + 1 - width)
    col_term = (2 * col_index + 1 - width) * (2 * col_index + 1 - width)
    return (row_term[:, None] + col_term[None, :] < width * width).astype(jnp.float32)

def product(left, right):
    return jnp.dot(left, right, preferred_element_type=jnp.float32)

def one_window(spec_re, spec_im, row_start, col_start, image, cos_table, sin_table, mask):
    win_re = (lax.dynamic_slice(spec_re, (row_start, col_start), (WIN, WIN)) * mask).astype(jnp.bfloat16)
    win_im = (lax.dynamic_slice(spec_im, (row_start, col_start), (WIN, WIN)) * mask).astype(jnp.bfloat16)
    row_re = (product(win_re, cos_table) + product(win_im, sin_table)).astype(jnp.bfloat16)
    row_im = (product(win_im, cos_table) - product(win_re, sin_table)).astype(jnp.bfloat16)
    field_re = product(row_re.T, cos_table) + product(row_im.T, sin_table)
    field_im = product(row_im.T, cos_table) - product(row_re.T, sin_table)
    factor = jnp.sqrt(image) / jnp.sqrt(field_re * field_re + field_im * field_im + 0.25) - 1.0
    diff_re = (field_re * factor).astype(jnp.bfloat16)
    diff_im = (field_im * factor).astype(jnp.bfloat16)
    back_re = (product(diff_re, cos_table) - product(diff_im, sin_table)).astype(jnp.bfloat16)
    back_im = (product(diff_im, cos_table) + product(diff_re, sin_table)).astype(jnp.bfloat16)
    upd_re = product(back_re.T, cos_table) - product(back_im.T, sin_table)
    upd_im = product(back_im.T, cos_table) + product(back_re.T, sin_table)
    return (upd_re * mask, upd_im * mask)

def reference(spectrum, led_rows, led_cols, images):
    cos_table, sin_table = make_tables(WIN)
    index = jnp.arange(WIN, dtype=jnp.int32)
    mask = make_pupil(index, index, WIN)
    spec_re = spectrum[0]
    spec_im = spectrum[1]
    grad_re = jnp.zeros((NROW, NCOL), jnp.float32)
    grad_im = jnp.zeros((NROW, NCOL), jnp.float32)
    for number in range(LEDS):
        row_start = led_rows[number].astype(jnp.int32)
        col_start = led_cols[number].astype(jnp.int32)
        upd_re, upd_im = one_window(spec_re, spec_im, row_start, col_start, images[number], cos_table, sin_table, mask)
        current_re = lax.dynamic_slice(grad_re, (row_start, col_start), (WIN, WIN))
        current_im = lax.dynamic_slice(grad_im, (row_start, col_start), (WIN, WIN))
        grad_re = lax.dynamic_update_slice(grad_re, current_re + upd_re, (row_start, col_start))
        grad_im = lax.dynamic_update_slice(grad_im, current_im + upd_im, (row_start, col_start))
    return spectrum + jnp.stack([grad_re, grad_im])
```

```python
import functools

import jax
import jax.numpy as jnp
import numpy as np
from jax import lax
from jax.experimental import pallas as pl
from jax.experimental.pallas import tpu as pltpu
from jax.sharding import PartitionSpec as P

NY, NZ, NC, NX = 4, 16, 2, 4
WIN = 1024
MESH = pl.DeviceIdType.MESH
F32, BF16 = jnp.float32, jnp.bfloat16


def grid_of(*sizes):
    return np.meshgrid(*[np.arange(n) for n in sizes], indexing="ij")


def rotation(angle_index, period, out_part, in_part, sign):
    angle = 2.0 * np.pi * (angle_index % period) / period
    same = np.cos(angle)
    cross = sign * np.sin(angle)
    return np.where(out_part == in_part, same, np.where(out_part == 1, cross, -cross))


def split(table):
    high = np.asarray(table, np.float32).astype(BF16)
    low = (table - high.astype(np.float64)).astype(np.float32).astype(BF16)
    return high, low


def make_tables():
    scale = 1.0 / 32.0
    y, c, po, z, pi, n2 = grid_of(NY, NC, 2, NZ, 2, 128)
    k2 = (y * NZ + z) * NC + c
    cols_fwd = scale * rotation(k2 * n2, 128, po, pi, -1).reshape(256, 256)
    z, l, yb, c, p, y2, c2, l2, p2, z2 = grid_of(NZ, 2, 2, NC, 2, NY, NC, 2, 2, NZ)
    hit = (z == z2) & (l == l2) & (p == p2) & (c == c2) & (y2 % 2 == yb)
    fold = hit.astype(np.float64).reshape(256, 512)
    l, po, p, z, l2, yb, c, pi = grid_of(2, 2, 64, NZ, 2, 2, NC, 2)
    strip = 32 * yb + 2 * z + c
    rows_fwd = (scale * rotation(strip * p, 64, po, pi, -1) * (l == l2)).reshape(256, 256)
    z, l, yb, c, po, l2, pi, p = grid_of(NZ, 2, 2, NC, 2, 2, 2, 64)
    strip = 32 * yb + 2 * z + c
    rows_inv = (scale * rotation(strip * p, 64, po, pi, 1) * (l == l2)).reshape(256, 256)
    pi, k1, i, po, q, k1o = grid_of(2, 8, 16, 2, 16, 8)
    short_fwd = (rotation(i * q, 16, po, pi, -1) * (k1 == k1o)).reshape(256, 256)
    pi, q, k1, po, k1o, i = grid_of(2, 16, 8, 2, 8, 16)
    short_inv = (rotation(i * q, 16, po, pi, 1) * (k1 == k1o)).reshape(256, 256)
    yb, c, l, p, z, z2, l2, yb2, c2, p2 = grid_of(2, NC, 2, 2, NZ, NZ, 2, 2, NC, 2)
    hit = (z == z2) & (l == l2) & (p == p2) & (c == c2) & (yb == yb2)
    swap = hit.astype(np.float64).reshape(256, 256)
    po, n2, y, c, pi, z = grid_of(2, 128, NY, NC, 2, NZ)
    k2 = (y * NZ + z) * NC + c
    cols_inv = scale * rotation(k2 * n2, 128, po, pi, 1).reshape(256, 256)
    halves = []
    for table in (cols_fwd, rows_fwd, short_fwd, short_inv, rows_inv, cols_inv):
        halves.extend(split(table))
    moves = [fold[:, :256], fold[:, 256:], swap]
    stack = np.stack(halves + [np.asarray(m, np.float32).astype(BF16) for m in moves])
    k1, n2 = grid_of(8, 128)
    angle = 2.0 * np.pi * ((k1 * n2) % WIN) / WIN
    twist_cols = np.stack([np.cos(angle), np.sin(angle)]).astype(np.float32)
    p, k1, i = grid_of(64, 8, 16)
    angle = (2.0 * np.pi * ((p * i) % WIN) / WIN).reshape(64, 128)
    twist_rows = np.stack([np.cos(angle), np.sin(angle)]).astype(np.float32)
    return stack, twist_cols, twist_rows


COLS_FWD, ROWS_FWD, SHORT_FWD, SHORT_INV, ROWS_INV, COLS_INV = range(0, 12, 2)
FOLD, SWAP = 12, 14


def fft(values, sign):
    size = len(values)
    if size == 1:
        return values
    even, odd = fft(values[0::2], sign), fft(values[1::2], sign)
    low, high = [], []
    for k in range(size // 2):
        (er, ei), (re, im) = even[k], odd[k]
        if k == 0:
            tr, ti = re, im
        elif 4 * k == size:
            tr, ti = (-im, re) if sign > 0 else (im, -re)
        else:
            a = float(np.cos(2 * np.pi * k / size))
            b = float(np.sin(2 * np.pi * k / size)) * sign
            tr, ti = a * re - b * im, a * im + b * re
        low.append((er + tr, ei + ti))
        high.append((er - tr, ei - ti))
    return low + high


def halves(value):
    high = value.astype(BF16)
    return high, (value - high.astype(F32)).astype(BF16)


def dot(left, right, right_dim=0):
    return lax.dot_general(
        left, right, (((1,), (right_dim,)), ((), ())), preferred_element_type=F32
    )


def dot_left(tables, at, value, right_dim=0):
    high, low = halves(value)
    return (
        dot(tables[at], high, right_dim)
        + dot(tables[at + 1], high, right_dim)
        + dot(tables[at], low, right_dim)
    )


def dot_right(value, tables, at):
    high, low = halves(value)
    return dot(high, tables[at]) + dot(low, tables[at]) + dot(high, tables[at + 1])


def step_kernel(
    led_rows, led_cols, spectrum, images, tables_in, twist_cols_in, twist_rows_in, out,
    spec, img, tables, twist_cols, twist_rows, grad,
    send1, recv1, send2, recv2, send3, recv3, send4, recv4, send5, recv5,
    in_sem, s1, r1, s2, r2, s3, r3, s4, r4, s5, r5,
):
    slab, led = lax.axis_index("slab"), lax.axis_index("led")
    core = lax.rem(slab, NC)
    z = lax.rem(lax.div(slab, NC), NZ)
    y = lax.div(slab, NC * NZ)
    yc = y * NC + core

    def slab_of(ny, nz, nc):
        return (ny * NZ + nz) * NC + nc

    near = [(2, 1), (2, 0), (1, 1), (3, 1), (1, 0), (3, 0), (0, 1)]
    near = [(lax.rem(y + dy, NY), lax.rem(core + dc, NC)) for dy, dc in near]
    far = [8, 7, 9, 6, 10, 5, 11, 4, 12, 3, 13, 2, 14, 1, 15]
    far = [lax.rem(z + dz, NZ) for dz in far]
    across = [lax.rem(led + dx, NX) for dx in (2, 1, 3)]

    barrier = pltpu.get_barrier_semaphore()
    for nz in far:
        pl.semaphore_signal(
            barrier, inc=1, device_id=(slab_of(y, nz, core), led), device_id_type=MESH
        )
    for ny, nc in near:
        pl.semaphore_signal(
            barrier, inc=1, device_id=(slab_of(ny, z, nc), led), device_id_type=MESH
        )
    for nx in across:
        pl.semaphore_signal(barrier, inc=1, device_id=(slab, nx), device_id_type=MESH)

    loads = [
        pltpu.make_async_copy(a, b, in_sem.at[n])
        for n, (a, b) in enumerate(
            [
                (spectrum, spec),
                (twist_cols_in, twist_cols),
                (tables_in.at[0:2], tables.at[0:2]),
                (images, img),
                (twist_rows_in, twist_rows),
                (tables_in.at[2:15], tables.at[2:15]),
            ]
        )
    ]
    for load in loads:
        load.start()

    row_at = slab * 16 + lax.broadcasted_iota(jnp.int32, (16, 128), 0)
    lane = lax.broadcasted_iota(jnp.int32, (16, 128), 1)

    def term(offset):
        return (2 * offset + 1 - WIN) * (2 * offset + 1 - WIN)

    row_terms = [term(row_at - led_rows[l]) for l in range(2)]

    def inside(l, block):
        return row_terms[l] + term(lane + (block * 128 - led_cols[l])) < WIN * WIN

    for load in loads[:3]:
        load.wait()
    pieces = []
    for l in range(2):
        values = []
        masks = [inside(l, block) for block in range(16)]
        for n1 in range(8):
            parts = []
            for part in range(2):
                first = spec[part, :, n1 * 128 : n1 * 128 + 128]
                second = spec[part, :, 1024 + n1 * 128 : 1152 + n1 * 128]
                parts.append(
                    jnp.where(masks[n1], first, 0.0) + jnp.where(masks[n1 + 8], second, 0.0)
                )
            values.append(tuple(parts))
        for k1, (re, im) in enumerate(fft(values, -1)):
            a, b = twist_cols[0, k1 : k1 + 1, :], twist_cols[1, k1 : k1 + 1, :]
            pieces.append(jnp.concatenate([re * a + im * b, im * a - re * b], axis=1))
    result = dot_left(tables, COLS_FWD, jnp.concatenate(pieces, axis=0), 1).astype(BF16)
    for l in range(2):
        send1[:, l * 32 : l * 32 + 32, :] = result[:, l * 128 : l * 128 + 128].reshape(8, 32, 128)
    recv1[yc] = send1[yc]

    pl.semaphore_wait(barrier, len(far) + len(near) + len(across))

    def exchange_near(send, recv, slot_of, send_sem, recv_sem):
        copies = []
        for n, (ny, nc) in enumerate(near):
            copy = pltpu.make_async_remote_copy(
                src_ref=send.at[slot_of(ny, nc)],
                dst_ref=recv.at[yc],
                send_sem=send_sem.at[n],
                recv_sem=recv_sem.at[n],
                device_id=(slab_of(ny, z, nc), led),
                device_id_type=MESH,
            )
            copy.start()
            copies.append(copy)
        return copies

    def exchange_far(send, recv, send_sem, recv_sem):
        copies = []
        for n, nz in enumerate(far):
            copy = pltpu.make_async_remote_copy(
                src_ref=send.at[nz],
                dst_ref=recv.at[z],
                send_sem=send_sem.at[n],
                recv_sem=recv_sem.at[n],
                device_id=(slab_of(y, nz, core), led),
                device_id_type=MESH,
            )
            copy.start()
            copies.append(copy)
        return copies

    copies1 = exchange_near(send1, recv1, lambda ny, nc: ny * NC + nc, s1, r1)

    for load in loads[3:]:
        load.wait()
    moduli = []
    for l in range(2):
        stacked = jnp.concatenate(
            [img[l, :, q * 64 : q * 64 + 64] for q in range(16)], axis=0
        )
        moduli.append(jnp.sqrt(stacked).T)
    moduli = jnp.concatenate(moduli, axis=0)
    tw_re, tw_im = twist_rows[0], twist_rows[1]

    for copy in copies1:
        copy.wait_recv()
    moved = dot(tables[FOLD], recv1[0:4].reshape(256, 128)) + dot(
        tables[FOLD + 1], recv1[4:8].reshape(256, 128)
    )
    send2[...] = moved.astype(BF16).reshape(16, 16, 128)
    recv2[z] = send2[z]
    copies2 = exchange_far(send2, recv2, s2, r2)
    for copy in copies2:
        copy.wait_recv()

    strips = recv2[...].reshape(256, 128)
    mixed = dot(tables[ROWS_FWD], strips) + dot(tables[ROWS_FWD + 1], strips)
    rows = []
    for l in range(2):
        re, im = mixed[l * 128 : l * 128 + 64], mixed[l * 128 + 64 : l * 128 + 128]
        rows.append(
            jnp.concatenate([re * tw_re + im * tw_im, im * tw_re - re * tw_im], axis=1)
        )
    field = dot_right(jnp.concatenate(rows, axis=0), tables, SHORT_FWD)
    field_re, field_im = field[:, :128], field[:, 128:]
    factor = moduli / jnp.sqrt(field_re * field_re + field_im * field_im + 0.25) - 1.0
    change = jnp.concatenate([field_re * factor, field_im * factor], axis=1)
    back = dot_right(change, tables, SHORT_INV)
    rows = []
    for l in range(2):
        re, im = back[l * 64 : l * 64 + 64, :128], back[l * 64 : l * 64 + 64, 128:]
        rows.append(re * tw_re - im * tw_im)
        rows.append(im * tw_re + re * tw_im)
    result = dot_left(tables, ROWS_INV, jnp.concatenate(rows, axis=0))
    send3[...] = result.astype(BF16).reshape(16, 16, 128)
    recv3[z] = send3[z]
    copies3 = exchange_far(send3, recv3, s3, r3)
    for copy in copies3:
        copy.wait_recv()

    moved = dot(tables[SWAP], recv3[...].reshape(256, 128))
    send4[...] = moved.astype(BF16).reshape(4, 64, 128)
    own_slot = lax.rem(y, 2) * NC + core
    recv4[yc] = send4[own_slot]
    copies4 = exchange_near(send4, recv4, lambda ny, nc: lax.rem(ny, 2) * NC + nc, s4, r4)
    for copy in copies4:
        copy.wait_recv()

    home = jnp.concatenate(
        [recv4[:, l * 32 : l * 32 + 32, :].reshape(256, 128) for l in range(2)], axis=1
    )
    spread = dot(tables[COLS_INV], home) + dot(tables[COLS_INV + 1], home)
    updates = []
    for l in range(2):
        re = spread[:128, l * 128 : l * 128 + 128].T
        im = spread[128:, l * 128 : l * 128 + 128].T
        values = []
        for k1 in range(8):
            a, b = twist_cols[0, k1 : k1 + 1, :], twist_cols[1, k1 : k1 + 1, :]
            kr, ki = re[k1 * 16 : k1 * 16 + 16], im[k1 * 16 : k1 * 16 + 16]
            values.append((kr * a - ki * b, ki * a + kr * b))
        updates.append(fft(values, 1))
    for block in range(16):
        masks = [inside(l, block) for l in range(2)]
        for part in range(2):
            total = jnp.where(masks[0], updates[0][block % 8][part], 0.0) + jnp.where(
                masks[1], updates[1][block % 8][part], 0.0
            )
            lanes = slice(block % 4 * 128, block % 4 * 128 + 128)
            grad[block // 4, part, :, lanes] = total
            send5[block // 4, part, :, lanes] = total.astype(BF16)
    copies5 = []
    for n, nx in enumerate(across):
        copy = pltpu.make_async_remote_copy(
            src_ref=send5.at[nx],
            dst_ref=recv5.at[n],
            send_sem=s5.at[n],
            recv_sem=r5.at[n],
            device_id=(slab, nx),
            device_id_type=MESH,
        )
        copy.start()
        copies5.append(copy)
    share = out.shape[2]
    total = spec[:, :, pl.ds(pl.multiple_of(led * share, share), share)] + grad[led]
    for n, copy in enumerate(copies5):
        copy.wait_recv()
    for n in range(3):
        total = total + recv5[n].astype(F32)
    out[...] = total
    for copy in copies1 + copies2 + copies3 + copies4 + copies5:
        copy.wait_send()


def body(tables, twist_cols, twist_rows, spectrum, led_rows, led_cols, images):
    smem = pl.BlockSpec(memory_space=pltpu.SMEM)
    here = pl.BlockSpec(memory_space=pl.ANY)
    columns = spectrum.shape[2]
    share = columns // NX
    return pl.pallas_call(
        step_kernel,
        out_shape=jax.ShapeDtypeStruct((2, 16, share), F32),
        in_specs=[smem, smem] + [here] * 5,
        out_specs=pl.BlockSpec(memory_space=pltpu.VMEM),
        scratch_shapes=[
            pltpu.VMEM((2, 16, columns), F32),
            pltpu.VMEM((2, 8, WIN), F32),
            pltpu.VMEM(tables.shape, BF16),
            pltpu.VMEM(twist_cols.shape, F32),
            pltpu.VMEM(twist_rows.shape, F32),
            pltpu.VMEM((NX, 2, 16, share), F32),
            pltpu.VMEM((8, 64, 128), BF16),
            pltpu.VMEM((8, 64, 128), BF16),
            pltpu.VMEM((16, 16, 128), BF16),
            pltpu.VMEM((16, 16, 128), BF16),
            pltpu.VMEM((16, 16, 128), BF16),
            pltpu.VMEM((16, 16, 128), BF16),
            pltpu.VMEM((4, 64, 128), BF16),
            pltpu.VMEM((8, 64, 128), BF16),
            pltpu.VMEM((NX, 2, 16, share), BF16),
            pltpu.VMEM((3, 2, 16, share), BF16),
            pltpu.SemaphoreType.DMA((6,)),
        ]
        + [pltpu.SemaphoreType.DMA((n,)) for n in (7, 7, 15, 15, 15, 15, 7, 7, 3, 3)],
        compiler_params=pltpu.CompilerParams(collective_id=0, has_side_effects=True),
        name="ptychography_step",
    )(led_rows, led_cols, spectrum, images, tables, twist_cols, twist_rows)


def solution(mesh):
    tables = make_tables()
    placed = (P(None, "slab", None), P("led"), P("led"), P("led", "slab", None))
    mapped = jax.shard_map(
        body,
        mesh=mesh,
        in_specs=(P(), P(), P()) + placed,
        out_specs=P(None, "slab", "led"),
        check_vma=False,
    )

    def step(spectrum, led_rows, led_cols, images):
        constants = [jnp.asarray(table) for table in tables]
        return mapped(*constants, spectrum, led_rows, led_cols, images)

    return step
```

```python
import functools

import jax
import jax.numpy as jnp
import numpy as np
from jax import lax
from jax.experimental import pallas as pl
from jax.experimental.pallas import tpu as pltpu
from jax.sharding import PartitionSpec as P

NY, NZ, NC, NX = 4, 16, 2, 4
WIN = 1024
MESH = pl.DeviceIdType.MESH
F32, BF16 = jnp.float32, jnp.bfloat16


def grid_of(*sizes):
    return np.meshgrid(*[np.arange(n) for n in sizes], indexing="ij")


def rotation(angle_index, period, out_part, in_part, sign):
    angle = 2.0 * np.pi * (angle_index % period) / period
    same = np.cos(angle)
    cross = sign * np.sin(angle)
    return np.where(out_part == in_part, same, np.where(out_part == 1, cross, -cross))


def split(table):
    high = np.asarray(table, np.float32).astype(BF16)
    low = (table - high.astype(np.float64)).astype(np.float32).astype(BF16)
    return high, low


def make_tables():
    scale = 1.0 / 32.0
    y, c, po, z, pi, n2 = grid_of(NY, NC, 2, NZ, 2, 128)
    k2 = (y * NZ + z) * NC + c
    cols_fwd = scale * rotation(k2 * n2, 128, po, pi, -1).reshape(256, 256)
    z, l, yb, c, p, y2, c2, l2, p2, z2 = grid_of(NZ, 2, 2, NC, 2, NY, NC, 2, 2, NZ)
    hit = (z == z2) & (l == l2) & (p == p2) & (c == c2) & (y2 % 2 == yb)
    fold = hit.astype(np.float64).reshape(256, 512)
    l, po, p, z, l2, yb, c, pi = grid_of(2, 2, 64, NZ, 2, 2, NC, 2)
    strip = 32 * yb + 2 * z + c
    rows_fwd = (scale * rotation(strip * p, 64, po, pi, -1) * (l == l2)).reshape(256, 256)
    z, l, yb, c, po, l2, pi, p = grid_of(NZ, 2, 2, NC, 2, 2, 2, 64)
    strip = 32 * yb + 2 * z + c
    rows_inv = (scale * rotation(strip * p, 64, po, pi, 1) * (l == l2)).reshape(256, 256)
    pi, k1, i, po, q, k1o = grid_of(2, 8, 16, 2, 16, 8)
    short_fwd = (rotation(i * q, 16, po, pi, -1) * (k1 == k1o)).reshape(256, 256)
    pi, q, k1, po, k1o, i = grid_of(2, 16, 8, 2, 8, 16)
    short_inv = (rotation(i * q, 16, po, pi, 1) * (k1 == k1o)).reshape(256, 256)
    yb, c, l, p, z, z2, l2, yb2, c2, p2 = grid_of(2, NC, 2, 2, NZ, NZ, 2, 2, NC, 2)
    hit = (z == z2) & (l == l2) & (p == p2) & (c == c2) & (yb == yb2)
    swap = hit.astype(np.float64).reshape(256, 256)
    po, n2, y, c, pi, z = grid_of(2, 128, NY, NC, 2, NZ)
    k2 = (y * NZ + z) * NC + c
    cols_inv = scale * rotation(k2 * n2, 128, po, pi, 1).reshape(256, 256)
    halves = []
    for table in (cols_fwd, rows_fwd, short_fwd, short_inv, rows_inv, cols_inv):
        halves.extend(split(table))
    moves = [fold[:, :256], fold[:, 256:], swap]
    stack = np.stack(halves + [np.asarray(m, np.float32).astype(BF16) for m in moves])
    k1, n2 = grid_of(8, 128)
    angle = 2.0 * np.pi * ((k1 * n2) % WIN) / WIN
    twist_cols = np.stack([np.cos(angle), np.sin(angle)]).astype(np.float32)
    p, k1, i = grid_of(64, 8, 16)
    angle = (2.0 * np.pi * ((p * i) % WIN) / WIN).reshape(64, 128)
    twist_rows = np.stack([np.cos(angle), np.sin(angle)]).astype(np.float32)
    return stack, twist_cols, twist_rows


COLS_FWD, ROWS_FWD, SHORT_FWD, SHORT_INV, ROWS_INV, COLS_INV = range(0, 12, 2)
FOLD, SWAP = 12, 14


def fft(values, sign):
    size = len(values)
    if size == 1:
        return values
    even, odd = fft(values[0::2], sign), fft(values[1::2], sign)
    low, high = [], []
    for k in range(size // 2):
        (er, ei), (re, im) = even[k], odd[k]
        if k == 0:
            tr, ti = re, im
        elif 4 * k == size:
            tr, ti = (-im, re) if sign > 0 else (im, -re)
        else:
            a = float(np.cos(2 * np.pi * k / size))
            b = float(np.sin(2 * np.pi * k / size)) * sign
            tr, ti = a * re - b * im, a * im + b * re
        low.append((er + tr, ei + ti))
        high.append((er - tr, ei - ti))
    return low + high


def halves(value):
    high = value.astype(BF16)
    return high, (value - high.astype(F32)).astype(BF16)


def dot(left, right, right_dim=0):
    return lax.dot_general(
        left, right, (((1,), (right_dim,)), ((), ())), preferred_element_type=F32
    )


def dot_left(tables, at, value, right_dim=0):
    high, low = halves(value)
    return (
        dot(tables[at], high, right_dim)
        + dot(tables[at + 1], high, right_dim)
        + dot(tables[at], low, right_dim)
    )


def dot_right(value, tables, at):
    high, low = halves(value)
    return dot(high, tables[at]) + dot(low, tables[at]) + dot(high, tables[at + 1])


def step_kernel(
    rows_in, cols_in, spectrum, images, tables_in, twist_cols_in, twist_rows_in, out,
    led_rows, led_cols, spec, img, tables, twist_cols, twist_rows, grad,
    send1, recv1, send2, recv2, send3, recv3, send4, recv4, send5, recv5,
    in_sem, s1, r1, s2, r2, s3, r3, s4, r4, s5, r5,
):
    slab, led = lax.axis_index("slab"), lax.axis_index("led")
    core = lax.rem(slab, NC)
    z = lax.rem(lax.div(slab, NC), NZ)
    y = lax.div(slab, NC * NZ)
    yc = y * NC + core

    def slab_of(ny, nz, nc):
        return (ny * NZ + nz) * NC + nc

    near = [(2, 1), (2, 0), (1, 1), (3, 1), (1, 0), (3, 0), (0, 1)]
    near = [(lax.rem(y + dy, NY), lax.rem(core + dc, NC)) for dy, dc in near]
    far = [8, 7, 9, 6, 10, 5, 11, 4, 12, 3, 13, 2, 14, 1, 15]
    far = [lax.rem(z + dz, NZ) for dz in far]
    across = [lax.rem(led + dx, NX) for dx in (2, 1, 3)]

    loads = [
        pltpu.make_async_copy(a, b, in_sem.at[n])
        for n, (a, b) in enumerate(
            [
                (spectrum, spec),
                (rows_in, led_rows),
                (cols_in, led_cols),
                (twist_cols_in, twist_cols),
                (tables_in.at[0:2], tables.at[0:2]),
                (images, img),
                (twist_rows_in, twist_rows),
                (tables_in.at[2:15], tables.at[2:15]),
            ]
        )
    ]
    for load in loads:
        load.start()

    barrier = pltpu.get_barrier_semaphore()
    for nz in far:
        pl.semaphore_signal(
            barrier, inc=1, device_id=(slab_of(y, nz, core), led), device_id_type=MESH
        )
    for ny, nc in near:
        pl.semaphore_signal(
            barrier, inc=1, device_id=(slab_of(ny, z, nc), led), device_id_type=MESH
        )
    for nx in across:
        pl.semaphore_signal(barrier, inc=1, device_id=(slab, nx), device_id_type=MESH)

    row_at = slab * 16 + lax.broadcasted_iota(jnp.int32, (16, 128), 0)
    lane = lax.broadcasted_iota(jnp.int32, (16, 128), 1)

    def term(offset):
        return (2 * offset + 1 - WIN) * (2 * offset + 1 - WIN)

    def inside(l, block):
        return row_terms[l] + term(lane + (block * 128 - led_cols[l])) < WIN * WIN

    with jax.named_scope("wait_load"):
        for load in loads[:5]:
            load.wait()
    row_terms = [term(row_at - led_rows[l]) for l in range(2)]
    pieces = []
    for l in range(2):
        values = []
        masks = [inside(l, block) for block in range(16)]
        for n1 in range(8):
            parts = []
            for part in range(2):
                first = spec[part, :, n1 * 128 : n1 * 128 + 128]
                second = spec[part, :, 1024 + n1 * 128 : 1152 + n1 * 128]
                parts.append(
                    jnp.where(masks[n1], first, 0.0) + jnp.where(masks[n1 + 8], second, 0.0)
                )
            values.append(tuple(parts))
        for k1, (re, im) in enumerate(fft(values, -1)):
            a, b = twist_cols[0, k1 : k1 + 1, :], twist_cols[1, k1 : k1 + 1, :]
            pieces.append(jnp.concatenate([re * a + im * b, im * a - re * b], axis=1))
    result = dot_left(tables, COLS_FWD, jnp.concatenate(pieces, axis=0), 1).astype(BF16)
    for l in range(2):
        send1[:, l * 32 : l * 32 + 32, :] = result[:, l * 128 : l * 128 + 128].reshape(8, 32, 128)
    recv1[yc] = send1[yc]

    with jax.named_scope("wait_barrier"):
        pl.semaphore_wait(barrier, len(far) + len(near) + len(across))

    def exchange_near(send, recv, slot_of, send_sem, recv_sem):
        copies = []
        for n, (ny, nc) in enumerate(near):
            copy = pltpu.make_async_remote_copy(
                src_ref=send.at[slot_of(ny, nc)],
                dst_ref=recv.at[yc],
                send_sem=send_sem.at[n],
                recv_sem=recv_sem.at[n],
                device_id=(slab_of(ny, z, nc), led),
                device_id_type=MESH,
            )
            copy.start()
            copies.append(copy)
        return copies

    def exchange_far(send, recv, send_sem, recv_sem):
        copies = []
        for n, nz in enumerate(far):
            copy = pltpu.make_async_remote_copy(
                src_ref=send.at[nz],
                dst_ref=recv.at[z],
                send_sem=send_sem.at[n],
                recv_sem=recv_sem.at[n],
                device_id=(slab_of(y, nz, core), led),
                device_id_type=MESH,
            )
            copy.start()
            copies.append(copy)
        return copies

    copies1 = exchange_near(send1, recv1, lambda ny, nc: ny * NC + nc, s1, r1)

    for load in loads[5:]:
        load.wait()
    moduli = []
    for l in range(2):
        stacked = jnp.concatenate(
            [img[l, :, q * 64 : q * 64 + 64] for q in range(16)], axis=0
        )
        moduli.append(jnp.sqrt(stacked).T)
    moduli = jnp.concatenate(moduli, axis=0)
    tw_re, tw_im = twist_rows[0], twist_rows[1]

    with jax.named_scope("wait_1"):
        for copy in copies1:
            copy.wait_recv()
    moved = dot(tables[FOLD], recv1[0:4].reshape(256, 128)) + dot(
        tables[FOLD + 1], recv1[4:8].reshape(256, 128)
    )
    send2[...] = moved.astype(BF16).reshape(16, 16, 128)
    recv2[z] = send2[z]
    copies2 = exchange_far(send2, recv2, s2, r2)
    with jax.named_scope("wait_2"):
        for copy in copies2:
            copy.wait_recv()

    strips = recv2[...].reshape(256, 128)
    mixed = dot(tables[ROWS_FWD], strips) + dot(tables[ROWS_FWD + 1], strips)
    rows = []
    for l in range(2):
        re, im = mixed[l * 128 : l * 128 + 64], mixed[l * 128 + 64 : l * 128 + 128]
        rows.append(
            jnp.concatenate([re * tw_re + im * tw_im, im * tw_re - re * tw_im], axis=1)
        )
    field = dot_right(jnp.concatenate(rows, axis=0), tables, SHORT_FWD)
    field_re, field_im = field[:, :128], field[:, 128:]
    factor = moduli / jnp.sqrt(field_re * field_re + field_im * field_im + 0.25) - 1.0
    change = jnp.concatenate([field_re * factor, field_im * factor], axis=1)
    back = dot_right(change, tables, SHORT_INV)
    rows = []
    for l in range(2):
        re, im = back[l * 64 : l * 64 + 64, :128], back[l * 64 : l * 64 + 64, 128:]
        rows.append(re * tw_re - im * tw_im)
        rows.append(im * tw_re + re * tw_im)
    result = dot_left(tables, ROWS_INV, jnp.concatenate(rows, axis=0))
    send3[...] = result.astype(BF16).reshape(16, 16, 128)
    recv3[z] = send3[z]
    copies3 = exchange_far(send3, recv3, s3, r3)
    with jax.named_scope("wait_3"):
        for copy in copies3:
            copy.wait_recv()

    moved = dot(tables[SWAP], recv3[...].reshape(256, 128))
    send4[...] = moved.astype(BF16).reshape(4, 64, 128)
    own_slot = lax.rem(y, 2) * NC + core
    recv4[yc] = send4[own_slot]
    copies4 = exchange_near(send4, recv4, lambda ny, nc: lax.rem(ny, 2) * NC + nc, s4, r4)
    with jax.named_scope("wait_4"):
        for copy in copies4:
            copy.wait_recv()

    home = jnp.concatenate(
        [recv4[:, l * 32 : l * 32 + 32, :].reshape(256, 128) for l in range(2)], axis=1
    )
    spread = dot(tables[COLS_INV], home) + dot(tables[COLS_INV + 1], home)
    updates = []
    for l in range(2):
        re = spread[:128, l * 128 : l * 128 + 128].T
        im = spread[128:, l * 128 : l * 128 + 128].T
        values = []
        for k1 in range(8):
            a, b = twist_cols[0, k1 : k1 + 1, :], twist_cols[1, k1 : k1 + 1, :]
            kr, ki = re[k1 * 16 : k1 * 16 + 16], im[k1 * 16 : k1 * 16 + 16]
            values.append((kr * a - ki * b, ki * a + kr * b))
        updates.append(fft(values, 1))
    for block in range(16):
        masks = [inside(l, block) for l in range(2)]
        for part in range(2):
            total = jnp.where(masks[0], updates[0][block % 8][part], 0.0) + jnp.where(
                masks[1], updates[1][block % 8][part], 0.0
            )
            lanes = slice(block % 4 * 128, block % 4 * 128 + 128)
            grad[block // 4, part, :, lanes] = total
            send5[block // 4, part, :, lanes] = total.astype(BF16)
    copies5 = []
    for n, nx in enumerate(across):
        copy = pltpu.make_async_remote_copy(
            src_ref=send5.at[nx],
            dst_ref=recv5.at[n],
            send_sem=s5.at[n],
            recv_sem=r5.at[n],
            device_id=(slab, nx),
            device_id_type=MESH,
        )
        copy.start()
        copies5.append(copy)
    share = out.shape[2]
    total = spec[:, :, pl.ds(pl.multiple_of(led * share, share), share)] + grad[led]
    with jax.named_scope("wait_5"):
        for copy in copies5:
            copy.wait_recv()
    for n in range(3):
        total = total + recv5[n].astype(F32)
    out[...] = total
    for copy in copies1 + copies2 + copies3 + copies4 + copies5:
        copy.wait_send()


def body(tables, twist_cols, twist_rows, spectrum, led_rows, led_cols, images):
    here = pl.BlockSpec(memory_space=pl.ANY)
    columns = spectrum.shape[2]
    share = columns // NX
    return pl.pallas_call(
        step_kernel,
        out_shape=pltpu.VMEM((2, 16, share), F32),
        in_specs=[here] * 7,
        out_specs=pl.BlockSpec(memory_space=pltpu.VMEM),
        scratch_shapes=[
            pltpu.SMEM((2,), jnp.int32),
            pltpu.SMEM((2,), jnp.int32),
            pltpu.VMEM((2, 16, columns), F32),
            pltpu.VMEM((2, 8, WIN), F32),
            pltpu.VMEM(tables.shape, BF16),
            pltpu.VMEM(twist_cols.shape, F32),
            pltpu.VMEM(twist_rows.shape, F32),
            pltpu.VMEM((NX, 2, 16, share), F32),
            pltpu.VMEM((8, 64, 128), BF16),
            pltpu.VMEM((8, 64, 128), BF16),
            pltpu.VMEM((16, 16, 128), BF16),
            pltpu.VMEM((16, 16, 128), BF16),
            pltpu.VMEM((16, 16, 128), BF16),
            pltpu.VMEM((16, 16, 128), BF16),
            pltpu.VMEM((4, 64, 128), BF16),
            pltpu.VMEM((8, 64, 128), BF16),
            pltpu.VMEM((NX, 2, 16, share), BF16),
            pltpu.VMEM((3, 2, 16, share), BF16),
            pltpu.SemaphoreType.DMA((8,)),
        ]
        + [pltpu.SemaphoreType.DMA((n,)) for n in (7, 7, 15, 15, 15, 15, 7, 7, 3, 3)],
        compiler_params=pltpu.CompilerParams(collective_id=0, has_side_effects=True),
        name="ptychography_step",
    )(led_rows, led_cols, spectrum, images, tables, twist_cols, twist_rows)


def solution(mesh):
    tables = make_tables()
    placed = (P(None, "slab", None), P("led"), P("led"), P("led", "slab", None))
    mapped = jax.shard_map(
        body,
        mesh=mesh,
        in_specs=(P(), P(), P()) + placed,
        out_specs=P(None, "slab", "led"),
        check_vma=False,
    )

    def step(spectrum, led_rows, led_cols, images):
        constants = [jnp.asarray(table) for table in tables]
        return mapped(*constants, spectrum, led_rows, led_cols, images)

    return step
```

```python
import functools

import jax
import jax.numpy as jnp
import numpy as np
from jax import lax
from jax.experimental import pallas as pl
from jax.experimental.pallas import tpu as pltpu
from jax.sharding import PartitionSpec as P

NY, NZ, NC, NX = 4, 16, 2, 4
WIN = 1024
MESH = pl.DeviceIdType.MESH
F32, BF16 = jnp.float32, jnp.bfloat16


def grid_of(*sizes):
    return np.meshgrid(*[np.arange(n) for n in sizes], indexing="ij")


def rotation(angle_index, period, out_part, in_part, sign):
    angle = 2.0 * np.pi * (angle_index % period) / period
    same = np.cos(angle)
    cross = sign * np.sin(angle)
    return np.where(out_part == in_part, same, np.where(out_part == 1, cross, -cross))


def split(table):
    high = np.asarray(table, np.float32).astype(BF16)
    low = (table - high.astype(np.float64)).astype(np.float32).astype(BF16)
    return high, low


def make_tables():
    scale = 1.0 / 32.0
    y, c, po, z, pi, n2 = grid_of(NY, NC, 2, NZ, 2, 128)
    k2 = (y * NZ + z) * NC + c
    cols_fwd = scale * rotation(k2 * n2, 128, po, pi, -1).reshape(256, 256)
    z, yb, c, p, y2, c2, p2, z2 = grid_of(NZ, 2, NC, 2, NY, NC, 2, NZ)
    hit = (z == z2) & (p == p2) & (c == c2) & (y2 % 2 == yb)
    fold = hit.astype(np.float64).reshape(128, 256)
    po, p, z, yb, c, pi = grid_of(2, 64, NZ, 2, NC, 2)
    strip = 32 * yb + 2 * z + c
    rows_fwd = scale * rotation(strip * p, 64, po, pi, -1).reshape(128, 128)
    z, yb, c, po, pi, p = grid_of(NZ, 2, NC, 2, 2, 64)
    strip = 32 * yb + 2 * z + c
    rows_inv = scale * rotation(strip * p, 64, po, pi, 1).reshape(128, 128)
    pi, k1, i, po, q, k1o = grid_of(2, 8, 16, 2, 16, 8)
    short_fwd = (rotation(i * q, 16, po, pi, -1) * (k1 == k1o)).reshape(256, 256)
    pi, q, k1, po, k1o, i = grid_of(2, 16, 8, 2, 8, 16)
    short_inv = (rotation(i * q, 16, po, pi, 1) * (k1 == k1o)).reshape(256, 256)
    yb, c, p, z, z2, yb2, c2, p2 = grid_of(2, NC, 2, NZ, NZ, 2, NC, 2)
    hit = (z == z2) & (p == p2) & (c == c2) & (yb == yb2)
    swap = hit.astype(np.float64).reshape(128, 128)
    po, n2, y, c, pi, z = grid_of(2, 128, NY, NC, 2, NZ)
    k2 = (y * NZ + z) * NC + c
    cols_inv = scale * rotation(k2 * n2, 128, po, pi, 1).reshape(256, 256)
    wide, small = [], []
    for table in (cols_fwd, short_fwd, short_inv, cols_inv):
        wide.extend(split(table))
    for table in (rows_fwd, rows_inv):
        small.extend(split(table))
    for table in (fold[:, :128], fold[:, 128:], swap):
        small.append(np.asarray(table, np.float32).astype(BF16))
    k1, n2 = grid_of(8, 128)
    angle = 2.0 * np.pi * ((k1 * n2) % WIN) / WIN
    twist_cols = np.stack([np.cos(angle), np.sin(angle)]).astype(np.float32)
    p, k1, i = grid_of(64, 8, 16)
    angle = (2.0 * np.pi * ((p * i) % WIN) / WIN).reshape(64, 128)
    twist_rows = np.stack([np.cos(angle), np.sin(angle)]).astype(np.float32)
    return np.stack(wide), np.stack(small), twist_cols, twist_rows


COLS_FWD, SHORT_FWD, SHORT_INV, COLS_INV = range(0, 8, 2)
ROWS_FWD, ROWS_INV, FOLD, SWAP = 0, 2, 4, 6
LINKS = (1, 3, 4)


def fft(values, sign):
    size = len(values)
    if size == 1:
        return values
    even, odd = fft(values[0::2], sign), fft(values[1::2], sign)
    low, high = [], []
    for k in range(size // 2):
        (er, ei), (re, im) = even[k], odd[k]
        if k == 0:
            tr, ti = re, im
        elif 4 * k == size:
            tr, ti = (-im, re) if sign > 0 else (im, -re)
        else:
            a = float(np.cos(2 * np.pi * k / size))
            b = float(np.sin(2 * np.pi * k / size)) * sign
            tr, ti = a * re - b * im, a * im + b * re
        low.append((er + tr, ei + ti))
        high.append((er - tr, ei - ti))
    return low + high


def halves(value):
    high = value.astype(BF16)
    return high, (value - high.astype(F32)).astype(BF16)


def dot(left, right, right_dim=0):
    return lax.dot_general(
        left, right, (((1,), (right_dim,)), ((), ())), preferred_element_type=F32
    )


def dot_left(tables, at, value, right_dim=0):
    high, low = halves(value)
    return (
        dot(tables[at], high, right_dim)
        + dot(tables[at + 1], high, right_dim)
        + dot(tables[at], low, right_dim)
    )


def dot_right(value, tables, at):
    high, low = halves(value)
    return dot(high, tables[at]) + dot(low, tables[at]) + dot(high, tables[at + 1])


def step_kernel(
    rows_in, cols_in, spectrum, images, wide_in, small_in, twist_cols_in, twist_rows_in, out,
    led_rows, led_cols, spec, img, wide, small, twist_cols, twist_rows, grad,
    send1, recv1, send2, recv2, send3, recv3, send4, recv4, send5, recv5,
    in_sem, known, s1, r1, s2, r2, s3, r3, s4, r4, s5, r5,
):
    slab, led = lax.axis_index("slab"), lax.axis_index("led")
    core = lax.rem(slab, NC)
    z = lax.rem(lax.div(slab, NC), NZ)
    y = lax.div(slab, NC * NZ)
    yc = y * NC + core

    def slab_of(ny, nz, nc):
        return (ny * NZ + nz) * NC + nc

    near = [(2, 1), (2, 0), (1, 1), (3, 1), (1, 0), (3, 0), (0, 1)]
    near = [(lax.rem(y + dy, NY), lax.rem(core + dc, NC)) for dy, dc in near]
    far = [8, 7, 9, 6, 10, 5, 11, 4, 12, 3, 13, 2, 14, 1, 15]
    far = [lax.rem(z + dz, NZ) for dz in far]
    links = [lax.rem(z + dz, NZ) for d in LINKS for dz in (d, NZ - d)]
    across = [lax.rem(led + dx, NX) for dx in (2, 1, 3)]

    loads = [
        pltpu.make_async_copy(a, b, in_sem.at[n])
        for n, (a, b) in enumerate(
            [
                (spectrum, spec),
                (rows_in, led_rows),
                (cols_in, led_cols),
                (twist_cols_in, twist_cols),
                (wide_in.at[0:2], wide.at[0:2]),
                (images, img),
                (twist_rows_in, twist_rows),
                (small_in, small),
                (wide_in.at[2:8], wide.at[2:8]),
            ]
        )
    ]
    for load in loads:
        load.start()
    barrier = pltpu.get_barrier_semaphore()

    def greet_links(semaphore):
        for nz in links:
            pl.semaphore_signal(
                semaphore, inc=1, device_id=(slab_of(y, nz, core), led), device_id_type=MESH
            )

    greet_links(barrier)
    for ny, nc in near:
        pl.semaphore_signal(
            barrier, inc=1, device_id=(slab_of(ny, z, nc), led), device_id_type=MESH
        )
    for nx in across:
        pl.semaphore_signal(barrier, inc=1, device_id=(slab, nx), device_id_type=MESH)

    row_at = slab * 16 + lax.broadcasted_iota(jnp.int32, (16, 128), 0)
    lane = lax.broadcasted_iota(jnp.int32, (16, 128), 1)

    def term(offset):
        return (2 * offset + 1 - WIN) * (2 * offset + 1 - WIN)

    def inside(l, block):
        return row_terms[l] + term(lane + (block * 128 - led_cols[l])) < WIN * WIN

    def exchange(n_peers, source_of, target, peer_of, send_sem, recv_sem):
        copies = []
        for n in range(n_peers):
            copy = pltpu.make_async_remote_copy(
                src_ref=source_of(n),
                dst_ref=target(n),
                send_sem=send_sem.at[n],
                recv_sem=recv_sem.at[n],
                device_id=peer_of(n),
                device_id_type=MESH,
            )
            copy.start()
            copies.append(copy)
        return copies

    def near_peer(n):
        ny, nc = near[n]
        return slab_of(ny, z, nc), led

    def far_peer(n):
        return slab_of(y, far[n], core), led

    def arrived(name, copies):
        with jax.named_scope(name):
            for copy in copies:
                copy.wait_recv()

    with jax.named_scope("wait_load"):
        for load in loads[:5]:
            load.wait()
    row_terms = [term(row_at - led_rows[l]) for l in range(2)]
    for l in range(2):
        pieces = []
        values = []
        masks = [inside(l, block) for block in range(16)]
        for n1 in range(8):
            parts = []
            for part in range(2):
                first = spec[part, :, n1 * 128 : n1 * 128 + 128]
                second = spec[part, :, 1024 + n1 * 128 : 1152 + n1 * 128]
                parts.append(
                    jnp.where(masks[n1], first, 0.0) + jnp.where(masks[n1 + 8], second, 0.0)
                )
            values.append(tuple(parts))
        for k1, (re, im) in enumerate(fft(values, -1)):
            a, b = twist_cols[0, k1 : k1 + 1, :], twist_cols[1, k1 : k1 + 1, :]
            pieces.append(jnp.concatenate([re * a + im * b, im * a - re * b], axis=1))
        result = dot_left(wide, COLS_FWD, jnp.concatenate(pieces, axis=0), 1)
        send1[l] = result.astype(BF16).reshape(8, 32, 128)
        recv1[l, yc] = send1[l, yc]

    with jax.named_scope("wait_barrier"):
        pl.semaphore_wait(barrier, len(links) + len(near) + len(across))
    greet_links(known)
    copies1 = [
        exchange(
            len(near),
            lambda n: send1.at[l, near[n][0] * NC + near[n][1]],
            lambda n: recv1.at[l, yc],
            near_peer,
            s1.at[l],
            r1.at[l],
        )
        for l in range(2)
    ]

    for load in loads[5:]:
        load.wait()
    moduli = []
    for l in range(2):
        stacked = jnp.concatenate(
            [img[l, :, q * 64 : q * 64 + 64] for q in range(16)], axis=0
        )
        moduli.append(jnp.sqrt(stacked).T)
    tw_re, tw_im = twist_rows[0], twist_rows[1]

    copies2 = []
    for l in range(2):
        arrived("wait_1%d" % l, copies1[l])
        moved = dot(small[FOLD], recv1[l, 0:4].reshape(128, 128)) + dot(
            small[FOLD + 1], recv1[l, 4:8].reshape(128, 128)
        )
        send2[l] = moved.astype(BF16).reshape(16, 8, 128)
        recv2[l, z] = send2[l, z]
        if l == 0:
            with jax.named_scope("wait_known"):
                pl.semaphore_wait(known, len(links))
        copies2.append(
            exchange(
                len(far),
                lambda n: send2.at[l, far[n]],
                lambda n: recv2.at[l, z],
                far_peer,
                s2.at[l],
                r2.at[l],
            )
        )

    copies3 = []
    for l in range(2):
        arrived("wait_2%d" % l, copies2[l])
        strips = recv2[l].reshape(128, 128)
        mixed = dot(small[ROWS_FWD], strips) + dot(small[ROWS_FWD + 1], strips)
        re, im = mixed[:64], mixed[64:]
        rows = jnp.concatenate([re * tw_re + im * tw_im, im * tw_re - re * tw_im], axis=1)
        field = dot_right(rows, wide, SHORT_FWD)
        field_re, field_im = field[:, :128], field[:, 128:]
        factor = moduli[l] / jnp.sqrt(field_re * field_re + field_im * field_im + 0.25) - 1.0
        change = jnp.concatenate([field_re * factor, field_im * factor], axis=1)
        back = dot_right(change, wide, SHORT_INV)
        re, im = back[:, :128], back[:, 128:]
        rows = jnp.concatenate([re * tw_re - im * tw_im, im * tw_re + re * tw_im], axis=0)
        result = dot_left(small, ROWS_INV, rows)
        send3[l] = result.astype(BF16).reshape(16, 8, 128)
        recv3[l, z] = send3[l, z]
        copies3.append(
            exchange(
                len(far),
                lambda n: send3.at[l, far[n]],
                lambda n: recv3.at[l, z],
                far_peer,
                s3.at[l],
                r3.at[l],
            )
        )

    copies4 = []
    for l in range(2):
        arrived("wait_3%d" % l, copies3[l])
        moved = dot(small[SWAP], recv3[l].reshape(128, 128))
        send4[l] = moved.astype(BF16).reshape(4, 32, 128)
        recv4[l, yc] = send4[l, lax.rem(y, 2) * NC + core]
        copies4.append(
            exchange(
                len(near),
                lambda n: send4.at[l, lax.rem(near[n][0], 2) * NC + near[n][1]],
                lambda n: recv4.at[l, yc],
                near_peer,
                s4.at[l],
                r4.at[l],
            )
        )

    updates = []
    for l in range(2):
        arrived("wait_4%d" % l, copies4[l])
        home = recv4[l].reshape(256, 128)
        spread = dot(wide[COLS_INV], home) + dot(wide[COLS_INV + 1], home)
        re, im = spread[:128].T, spread[128:].T
        values = []
        for k1 in range(8):
            a, b = twist_cols[0, k1 : k1 + 1, :], twist_cols[1, k1 : k1 + 1, :]
            kr, ki = re[k1 * 16 : k1 * 16 + 16], im[k1 * 16 : k1 * 16 + 16]
            values.append((kr * a - ki * b, ki * a + kr * b))
        updates.append(fft(values, 1))
    for block in range(16):
        masks = [inside(l, block) for l in range(2)]
        for part in range(2):
            total = jnp.where(masks[0], updates[0][block % 8][part], 0.0) + jnp.where(
                masks[1], updates[1][block % 8][part], 0.0
            )
            lanes = slice(block % 4 * 128, block % 4 * 128 + 128)
            grad[block // 4, part, :, lanes] = total
            send5[block // 4, part, :, lanes] = total.astype(BF16)
    copies5 = exchange(
        len(across),
        lambda n: send5.at[across[n]],
        lambda n: recv5.at[n],
        lambda n: (slab, across[n]),
        s5,
        r5,
    )
    share = out.shape[2]
    total = spec[:, :, pl.ds(pl.multiple_of(led * share, share), share)] + grad[led]
    arrived("wait_5", copies5)
    for n in range(3):
        total = total + recv5[n].astype(F32)
    out[...] = total
    for copies in copies1 + copies2 + copies3 + copies4 + [copies5]:
        for copy in copies:
            copy.wait_send()


def body(wide, small, twist_cols, twist_rows, spectrum, led_rows, led_cols, images):
    columns = spectrum.shape[2]
    share = columns // NX
    pairs = [(2, 7), (2, 15), (2, 15), (2, 7), (3,)]
    return pl.pallas_call(
        step_kernel,
        out_shape=pltpu.VMEM((2, 16, share), F32),
        in_specs=[pl.BlockSpec(memory_space=pl.ANY)] * 8,
        out_specs=pl.BlockSpec(memory_space=pltpu.VMEM),
        scratch_shapes=[
            pltpu.SMEM((2,), jnp.int32),
            pltpu.SMEM((2,), jnp.int32),
            pltpu.VMEM((2, 16, columns), F32),
            pltpu.VMEM((2, 8, WIN), F32),
            pltpu.VMEM(wide.shape, BF16),
            pltpu.VMEM(small.shape, BF16),
            pltpu.VMEM(twist_cols.shape, F32),
            pltpu.VMEM(twist_rows.shape, F32),
            pltpu.VMEM((NX, 2, 16, share), F32),
            pltpu.VMEM((2, 8, 32, 128), BF16),
            pltpu.VMEM((2, 8, 32, 128), BF16),
            pltpu.VMEM((2, 16, 8, 128), BF16),
            pltpu.VMEM((2, 16, 8, 128), BF16),
            pltpu.VMEM((2, 16, 8, 128), BF16),
            pltpu.VMEM((2, 16, 8, 128), BF16),
            pltpu.VMEM((2, 4, 32, 128), BF16),
            pltpu.VMEM((2, 8, 32, 128), BF16),
            pltpu.VMEM((NX, 2, 16, share), BF16),
            pltpu.VMEM((3, 2, 16, share), BF16),
            pltpu.SemaphoreType.DMA((9,)),
            pltpu.SemaphoreType.REGULAR,
        ]
        + [pltpu.SemaphoreType.DMA(shape) for shape in pairs for _ in range(2)],
        compiler_params=pltpu.CompilerParams(collective_id=0, has_side_effects=True),
        name="ptychography_step",
    )(led_rows, led_cols, spectrum, images, wide, small, twist_cols, twist_rows)


def solution(mesh):
    tables = make_tables()
    placed = (P(None, "slab", None), P("led"), P("led"), P("led", "slab", None))
    mapped = jax.shard_map(
        body,
        mesh=mesh,
        in_specs=(P(),) * 4 + placed,
        out_specs=P(None, "slab", "led"),
        check_vma=False,
    )

    def step(spectrum, led_rows, led_cols, images):
        constants = [jnp.asarray(table) for table in tables]
        return mapped(*constants, spectrum, led_rows, led_cols, images)

    return step
```

```python
import functools

import jax
import jax.numpy as jnp
import numpy as np
from jax import lax
from jax.experimental import pallas as pl
from jax.experimental.pallas import tpu as pltpu
from jax.sharding import PartitionSpec as P

NY, NZ, NC, NX = 4, 16, 2, 4
WIN = 1024
MESH = pl.DeviceIdType.MESH
F32, BF16 = jnp.float32, jnp.bfloat16


def grid_of(*sizes):
    return np.meshgrid(*[np.arange(n) for n in sizes], indexing="ij")


def rotation(angle_index, period, out_part, in_part, sign):
    angle = 2.0 * np.pi * (angle_index % period) / period
    same = np.cos(angle)
    cross = sign * np.sin(angle)
    return np.where(out_part == in_part, same, np.where(out_part == 1, cross, -cross))


def split(table):
    high = np.asarray(table, np.float32).astype(BF16)
    low = (table - high.astype(np.float64)).astype(np.float32).astype(BF16)
    return high, low


def make_tables():
    scale = 1.0 / 32.0
    y, c, po, z, pi, n2 = grid_of(NY, NC, 2, NZ, 2, 128)
    k2 = (y * NZ + z) * NC + c
    cols_fwd = scale * rotation(k2 * n2, 128, po, pi, -1).reshape(256, 256)
    z, l, yb, c, p, y2, c2, l2, p2, z2 = grid_of(NZ, 2, 2, NC, 2, NY, NC, 2, 2, NZ)
    hit = (z == z2) & (l == l2) & (p == p2) & (c == c2) & (y2 % 2 == yb)
    fold = hit.astype(np.float64).reshape(256, 512)
    l, po, p, z, l2, yb, c, pi = grid_of(2, 2, 64, NZ, 2, 2, NC, 2)
    strip = 32 * yb + 2 * z + c
    rows_fwd = (scale * rotation(strip * p, 64, po, pi, -1) * (l == l2)).reshape(256, 256)
    strip, l, po, l2, pi, p = grid_of(64, 2, 2, 2, 2, 64)
    rows_inv = (scale * rotation(strip * p, 64, po, pi, 1) * (l == l2)).reshape(256, 256)
    pi, k1, i, po, q, k1o = grid_of(2, 8, 16, 2, 16, 8)
    short_fwd = (rotation(i * q, 16, po, pi, -1) * (k1 == k1o)).reshape(256, 256)
    pi, q, k1, po, k1o, i = grid_of(2, 16, 8, 2, 8, 16)
    short_inv = (rotation(i * q, 16, po, pi, 1) * (k1 == k1o)).reshape(256, 256)
    l, po, n2, k2, l2, pi = grid_of(2, 2, 128, 128, 2, 2)
    cols_inv = (scale * rotation(k2 * n2, 128, po, pi, 1) * (l == l2)).reshape(512, 512)
    wide = []
    for table in (cols_fwd, short_fwd, short_inv, rows_fwd, rows_inv):
        wide.extend(split(table))
    for table in (fold[:, :256], fold[:, 256:]):
        wide.append(np.asarray(table, np.float32).astype(BF16))
    k1, n2 = grid_of(8, 128)
    angle = 2.0 * np.pi * ((k1 * n2) % WIN) / WIN
    twist_cols = np.stack([np.cos(angle), np.sin(angle)]).astype(np.float32)
    p, k1, i = grid_of(64, 8, 16)
    angle = (2.0 * np.pi * ((p * i) % WIN) / WIN).reshape(64, 128)
    twist_rows = np.stack([np.cos(angle), np.sin(angle)]).astype(np.float32)
    return np.stack(wide), np.stack(split(cols_inv)), twist_cols, twist_rows


COLS_FWD, SHORT_FWD, SHORT_INV, ROWS_FWD, ROWS_INV, FOLD = range(0, 12, 2)
LINKS = (1, 3, 4)
HOPS = sorted(
    ((dy, dz, dc) for dy in range(NY) for dz in range(NZ) for dc in range(NC)),
    key=lambda d: -(min(d[0], NY - d[0]) + min(d[1], NZ - d[1]) + 0.1 * d[2]),
)[:-1]


def fft(values, sign):
    size = len(values)
    if size == 1:
        return values
    even, odd = fft(values[0::2], sign), fft(values[1::2], sign)
    low, high = [], []
    for k in range(size // 2):
        (er, ei), (re, im) = even[k], odd[k]
        if k == 0:
            tr, ti = re, im
        elif 4 * k == size:
            tr, ti = (-im, re) if sign > 0 else (im, -re)
        else:
            a = float(np.cos(2 * np.pi * k / size))
            b = float(np.sin(2 * np.pi * k / size)) * sign
            tr, ti = a * re - b * im, a * im + b * re
        low.append((er + tr, ei + ti))
        high.append((er - tr, ei - ti))
    return low + high


def halves(value):
    high = value.astype(BF16)
    return high, (value - high.astype(F32)).astype(BF16)


def dot(left, right, right_dim=0):
    return lax.dot_general(
        left, right, (((1,), (right_dim,)), ((), ())), preferred_element_type=F32
    )


def dot_left(tables, at, value, right_dim=0):
    high, low = halves(value)
    return (
        dot(tables[at], high, right_dim)
        + dot(tables[at + 1], high, right_dim)
        + dot(tables[at], low, right_dim)
    )


def dot_right(value, tables, at):
    high, low = halves(value)
    return dot(high, tables[at]) + dot(low, tables[at]) + dot(high, tables[at + 1])


def step_kernel(
    rows_in, cols_in, spectrum, images, wide_in, cols_inv_in, twist_cols_in, twist_rows_in, out,
    led_rows, led_cols, spec, img, wide, cols_inv, twist_cols, twist_rows, grad,
    send1, recv1, send2, recv2, send3, recv3, send5, recv5,
    in_sem, known, sent, got,
):
    slab, led = lax.axis_index("slab"), lax.axis_index("led")
    core = lax.rem(slab, NC)
    z = lax.rem(lax.div(slab, NC), NZ)
    y = lax.div(slab, NC * NZ)
    yc = y * NC + core

    def slab_of(ny, nz, nc):
        return (ny * NZ + nz) * NC + nc

    near = [(2, 1), (2, 0), (1, 1), (3, 1), (1, 0), (3, 0), (0, 1)]
    near = [(lax.rem(y + dy, NY), lax.rem(core + dc, NC)) for dy, dc in near]
    far = [8, 7, 9, 6, 10, 5, 11, 4, 12, 3, 13, 2, 14, 1, 15]
    far = [lax.rem(z + dz, NZ) for dz in far]
    across = [lax.rem(led + dx, NX) for dx in (2, 1, 3)]

    loads = [
        pltpu.make_async_copy(a, b, in_sem.at[n])
        for n, (a, b) in enumerate(
            [
                (spectrum, spec),
                (rows_in, led_rows),
                (cols_in, led_cols),
                (twist_cols_in, twist_cols),
                (wide_in.at[0:2], wide.at[0:2]),
                (images, img),
                (twist_rows_in, twist_rows),
                (wide_in.at[2:12], wide.at[2:12]),
                (cols_inv_in, cols_inv),
            ]
        )
    ]
    for load in loads[:5]:
        load.start()
    barrier = pltpu.get_barrier_semaphore()

    links = [lax.rem(z + dz, NZ) for d in LINKS for dz in (d, NZ - d)]

    def greet_links(semaphore):
        for nz in links:
            pl.semaphore_signal(
                semaphore, inc=1, device_id=(slab_of(y, nz, core), led), device_id_type=MESH
            )

    greet_links(barrier)
    for ny, nc in near:
        pl.semaphore_signal(
            barrier, inc=1, device_id=(slab_of(ny, z, nc), led), device_id_type=MESH
        )
    for nx in across:
        pl.semaphore_signal(barrier, inc=1, device_id=(slab, nx), device_id_type=MESH)
    for load in loads[5:]:
        load.start()

    row_at = slab * 16 + lax.broadcasted_iota(jnp.int32, (16, 128), 0)
    lane = lax.broadcasted_iota(jnp.int32, (16, 128), 1)

    def term(offset):
        return (2 * offset + 1 - WIN) * (2 * offset + 1 - WIN)

    def inside(l, block):
        return row_terms[l] + term(lane + (block * 128 - led_cols[l])) < WIN * WIN

    def exchange(n_peers, source_of, target_of, peer_of, at):
        for n in range(n_peers):
            pltpu.make_async_remote_copy(
                src_ref=source_of(n),
                dst_ref=target_of(n),
                send_sem=sent.at[at],
                recv_sem=got.at[at],
                device_id=peer_of(n),
                device_id_type=MESH,
            ).start()

    def near_peer(n):
        ny, nc = near[n]
        return slab_of(ny, z, nc), led

    def far_peer(n):
        return slab_of(y, far[n], core), led

    def finish(semaphores, at, block):
        pltpu.make_async_copy(block, block, semaphores.at[at]).wait()

    with jax.named_scope("wait_load"):
        for load in loads[:5]:
            load.wait()
    row_terms = [term(row_at - led_rows[l]) for l in range(2)]
    pieces = []
    for l in range(2):
        values = []
        masks = [inside(l, block) for block in range(16)]
        for n1 in range(8):
            parts = []
            for part in range(2):
                first = spec[part, :, n1 * 128 : n1 * 128 + 128]
                second = spec[part, :, 1024 + n1 * 128 : 1152 + n1 * 128]
                parts.append(
                    jnp.where(masks[n1], first, 0.0) + jnp.where(masks[n1 + 8], second, 0.0)
                )
            values.append(tuple(parts))
        for k1, (re, im) in enumerate(fft(values, -1)):
            a, b = twist_cols[0, k1 : k1 + 1, :], twist_cols[1, k1 : k1 + 1, :]
            pieces.append(jnp.concatenate([re * a + im * b, im * a - re * b], axis=1))
    result = dot_left(wide, COLS_FWD, jnp.concatenate(pieces, axis=0), 1).astype(BF16)
    for l in range(2):
        send1[:, l * 32 : l * 32 + 32] = result[:, l * 128 : l * 128 + 128].reshape(8, 32, 128)
    recv1[yc] = send1[yc]

    with jax.named_scope("wait_barrier"):
        pl.semaphore_wait(barrier, len(links) + len(near) + len(across))
    greet_links(known)
    exchange(
        len(near),
        lambda n: send1.at[near[n][0] * NC + near[n][1]],
        lambda n: recv1.at[yc],
        near_peer,
        0,
    )

    for load in loads[5:]:
        load.wait()
    moduli = []
    for l in range(2):
        stacked = jnp.concatenate(
            [img[l, :, q * 64 : q * 64 + 64] for q in range(16)], axis=0
        )
        moduli.append(jnp.sqrt(stacked).T)
    moduli = jnp.concatenate(moduli, axis=0)
    tw_re, tw_im = twist_rows[0], twist_rows[1]

    with jax.named_scope("wait_1"):
        finish(got, 0, recv1.at[0:7])
    moved = dot(wide[FOLD], recv1[0:4].reshape(256, 128)) + dot(
        wide[FOLD + 1], recv1[4:8].reshape(256, 128)
    )
    send2[...] = moved.astype(BF16).reshape(16, 16, 128)
    recv2[z] = send2[z]
    with jax.named_scope("wait_known"):
        pl.semaphore_wait(known, len(links))
    exchange(
        len(far), lambda n: send2.at[far[n]], lambda n: recv2.at[z], far_peer, 1
    )

    with jax.named_scope("wait_2"):
        finish(got, 1, recv2.at[0:15])
    strips = recv2[...].reshape(256, 128)
    mixed = dot(wide[ROWS_FWD], strips) + dot(wide[ROWS_FWD + 1], strips)
    rows = []
    for l in range(2):
        re, im = mixed[l * 128 : l * 128 + 64], mixed[l * 128 + 64 : l * 128 + 128]
        rows.append(
            jnp.concatenate([re * tw_re + im * tw_im, im * tw_re - re * tw_im], axis=1)
        )
    field = dot_right(jnp.concatenate(rows, axis=0), wide, SHORT_FWD)
    field_re, field_im = field[:, :128], field[:, 128:]
    factor = moduli / jnp.sqrt(field_re * field_re + field_im * field_im + 0.25) - 1.0
    change = jnp.concatenate([field_re * factor, field_im * factor], axis=1)
    back = dot_right(change, wide, SHORT_INV)
    rows = []
    for l in range(2):
        re, im = back[l * 64 : l * 64 + 64, :128], back[l * 64 : l * 64 + 64, 128:]
        rows.append(re * tw_re - im * tw_im)
        rows.append(im * tw_re + re * tw_im)
    result = dot_left(wide, ROWS_INV, jnp.concatenate(rows, axis=0))
    send3[...] = result.astype(BF16).reshape(64, 4, 128)

    ys = [lax.rem(y + dy, NY) for dy in range(NY)]
    zs = [lax.rem(z + dz, NZ) * NC for dz in range(NZ)]
    cs = [core, NC - 1 - core]
    strips_of = [[lax.rem(y + dy, 2) * (NZ * NC) + zc for zc in zs] for dy in range(2)]
    exchange(
        len(HOPS),
        lambda n: send3.at[strips_of[HOPS[n][0] % 2][HOPS[n][1]] + cs[HOPS[n][2]]],
        lambda n: recv3.at[slab],
        lambda n: (ys[HOPS[n][0]] * (NZ * NC) + zs[HOPS[n][1]] + cs[HOPS[n][2]], led),
        2,
    )
    recv3[slab] = send3[lax.rem(slab, 64)]
    with jax.named_scope("wait_3"):
        finish(got, 2, recv3.at[0:127])

    home = recv3[...].reshape(512, 128)
    spread = dot(cols_inv[0], home) + dot(cols_inv[1], home)
    updates = []
    for l in range(2):
        re = spread[l * 256 : l * 256 + 128].T
        im = spread[l * 256 + 128 : l * 256 + 256].T
        values = []
        for k1 in range(8):
            a, b = twist_cols[0, k1 : k1 + 1, :], twist_cols[1, k1 : k1 + 1, :]
            kr, ki = re[k1 * 16 : k1 * 16 + 16], im[k1 * 16 : k1 * 16 + 16]
            values.append((kr * a - ki * b, ki * a + kr * b))
        updates.append(fft(values, 1))
    for block in range(16):
        masks = [inside(l, block) for l in range(2)]
        for part in range(2):
            total = jnp.where(masks[0], updates[0][block % 8][part], 0.0) + jnp.where(
                masks[1], updates[1][block % 8][part], 0.0
            )
            lanes = slice(block % 4 * 128, block % 4 * 128 + 128)
            grad[block // 4, part, :, lanes] = total
            send5[block // 4, part, :, lanes] = total.astype(BF16)
    exchange(
        len(across),
        lambda n: send5.at[across[n]],
        lambda n: recv5.at[n],
        lambda n: (slab, across[n]),
        3,
    )
    share = out.shape[2]
    total = spec[:, :, pl.ds(pl.multiple_of(led * share, share), share)] + grad[led]
    with jax.named_scope("wait_5"):
        finish(got, 3, recv5)
    for n in range(3):
        total = total + recv5[n].astype(F32)
    out[...] = total
    for at, block in enumerate([send1.at[0:7], send2.at[0:15], recv3.at[0:127], send5.at[0:3]]):
        finish(sent, at, block)


def body(wide, cols_inv, twist_cols, twist_rows, spectrum, led_rows, led_cols, images):
    columns = spectrum.shape[2]
    share = columns // NX
    return pl.pallas_call(
        step_kernel,
        out_shape=pltpu.VMEM((2, 16, share), F32),
        in_specs=[pl.BlockSpec(memory_space=pl.ANY)] * 8,
        out_specs=pl.BlockSpec(memory_space=pltpu.VMEM),
        scratch_shapes=[
            pltpu.SMEM((2,), jnp.int32),
            pltpu.SMEM((2,), jnp.int32),
            pltpu.VMEM((2, 16, columns), F32),
            pltpu.VMEM((2, 8, WIN), F32),
            pltpu.VMEM(wide.shape, BF16),
            pltpu.VMEM(cols_inv.shape, BF16),
            pltpu.VMEM(twist_cols.shape, F32),
            pltpu.VMEM(twist_rows.shape, F32),
            pltpu.VMEM((NX, 2, 16, share), F32),
            pltpu.VMEM((8, 64, 128), BF16),
            pltpu.VMEM((8, 64, 128), BF16),
            pltpu.VMEM((16, 16, 128), BF16),
            pltpu.VMEM((16, 16, 128), BF16),
            pltpu.VMEM((64, 4, 128), BF16),
            pltpu.VMEM((128, 4, 128), BF16),
            pltpu.VMEM((NX, 2, 16, share), BF16),
            pltpu.VMEM((3, 2, 16, share), BF16),
            pltpu.SemaphoreType.DMA((9,)),
            pltpu.SemaphoreType.REGULAR,
            pltpu.SemaphoreType.DMA((4,)),
            pltpu.SemaphoreType.DMA((4,)),
        ],
        compiler_params=pltpu.CompilerParams(collective_id=0, has_side_effects=True),
        name="ptychography_step",
    )(led_rows, led_cols, spectrum, images, wide, cols_inv, twist_cols, twist_rows)


def solution(mesh):
    tables = make_tables()
    placed = (P(None, "slab", None), P("led"), P("led"), P("led", "slab", None))
    mapped = jax.shard_map(
        body,
        mesh=mesh,
        in_specs=(P(),) * 4 + placed,
        out_specs=P(None, "slab", "led"),
        check_vma=False,
    )

    def step(spectrum, led_rows, led_cols, images):
        constants = [jnp.asarray(table) for table in tables]
        return mapped(*constants, spectrum, led_rows, led_cols, images)

    return step
```

```python
import functools

import jax
import jax.numpy as jnp
import numpy as np
from jax import lax
from jax.experimental import pallas as pl
from jax.experimental.pallas import tpu as pltpu
from jax.sharding import PartitionSpec as P

NY, NZ, NC, NX = 4, 16, 2, 4
WIN = 1024
MESH = pl.DeviceIdType.MESH
F32, BF16 = jnp.float32, jnp.bfloat16


def grid_of(*sizes):
    return np.meshgrid(*[np.arange(n) for n in sizes], indexing="ij")


def rotation(angle_index, period, out_part, in_part, sign):
    angle = 2.0 * np.pi * (angle_index % period) / period
    same = np.cos(angle)
    cross = sign * np.sin(angle)
    return np.where(out_part == in_part, same, np.where(out_part == 1, cross, -cross))


def split(table):
    high = np.asarray(table, np.float32).astype(BF16)
    low = (table - high.astype(np.float64)).astype(np.float32).astype(BF16)
    return high, low


def make_tables():
    scale = 1.0 / 32.0
    y, c, po, z, pi, n2 = grid_of(NY, NC, 2, NZ, 2, 128)
    k2 = (y * NZ + z) * NC + c
    cols_fwd = scale * rotation(k2 * n2, 128, po, pi, -1).reshape(256, 256)
    z, l, yb, c, p, y2, c2, l2, p2, z2 = grid_of(NZ, 2, 2, NC, 2, NY, NC, 2, 2, NZ)
    hit = (z == z2) & (l == l2) & (p == p2) & (c == c2) & (y2 % 2 == yb)
    fold = hit.astype(np.float64).reshape(256, 512)
    l, po, p, z, l2, yb, c, pi = grid_of(2, 2, 64, NZ, 2, 2, NC, 2)
    strip = 32 * yb + 2 * z + c
    rows_fwd = (scale * rotation(strip * p, 64, po, pi, -1) * (l == l2)).reshape(256, 256)
    strip, l, po, l2, pi, p = grid_of(64, 2, 2, 2, 2, 64)
    rows_inv = (scale * rotation(strip * p, 64, po, pi, 1) * (l == l2)).reshape(256, 256)
    pi, k1, i, po, q, k1o = grid_of(2, 8, 16, 2, 16, 8)
    short_fwd = (rotation(i * q, 16, po, pi, -1) * (k1 == k1o)).reshape(256, 256)
    pi, q, k1, po, k1o, i = grid_of(2, 16, 8, 2, 8, 16)
    short_inv = (rotation(i * q, 16, po, pi, 1) * (k1 == k1o)).reshape(256, 256)
    l, po, n2, k2, l2, pi = grid_of(2, 2, 128, 128, 2, 2)
    cols_inv = (scale * rotation(k2 * n2, 128, po, pi, 1) * (l == l2)).reshape(512, 512)
    wide = []
    for table in (cols_fwd, short_fwd, short_inv, rows_fwd, rows_inv):
        wide.extend(split(table))
    for table in (fold[:, :256], fold[:, 256:]):
        wide.append(np.asarray(table, np.float32).astype(BF16))
    k1, n2 = grid_of(8, 128)
    angle = 2.0 * np.pi * ((k1 * n2) % WIN) / WIN
    twist_cols = np.stack([np.cos(angle), np.sin(angle)]).astype(np.float32)
    p, k1, i = grid_of(64, 8, 16)
    angle = (2.0 * np.pi * ((p * i) % WIN) / WIN).reshape(64, 128)
    twist_rows = np.stack([np.cos(angle), np.sin(angle)]).astype(np.float32)
    return np.stack(wide), np.stack(split(cols_inv)), twist_cols, twist_rows


COLS_FWD, SHORT_FWD, SHORT_INV, ROWS_FWD, ROWS_INV, FOLD = range(0, 12, 2)
LINKS = (1, 3, 4)
FAR_FIRST = (8, 7, 9, 6, 10, 5, 11, 4, 12, 3, 13, 2, 14, 1, 15)


def fft(values, sign):
    size = len(values)
    if size == 1:
        return values
    even, odd = fft(values[0::2], sign), fft(values[1::2], sign)
    low, high = [], []
    for k in range(size // 2):
        (er, ei), (re, im) = even[k], odd[k]
        if k == 0:
            tr, ti = re, im
        elif 4 * k == size:
            tr, ti = (-im, re) if sign > 0 else (im, -re)
        else:
            a = float(np.cos(2 * np.pi * k / size))
            b = float(np.sin(2 * np.pi * k / size)) * sign
            tr, ti = a * re - b * im, a * im + b * re
        low.append((er + tr, ei + ti))
        high.append((er - tr, ei - ti))
    return low + high


def halves(value):
    high = value.astype(BF16)
    return high, (value - high.astype(F32)).astype(BF16)


def dot(left, right, right_dim=0):
    return lax.dot_general(
        left, right, (((1,), (right_dim,)), ((), ())), preferred_element_type=F32
    )


def dot_left(tables, at, value, right_dim=0):
    high, low = halves(value)
    return (
        dot(tables[at], high, right_dim)
        + dot(tables[at + 1], high, right_dim)
        + dot(tables[at], low, right_dim)
    )


def dot_right(value, tables, at):
    high, low = halves(value)
    return dot(high, tables[at]) + dot(low, tables[at]) + dot(high, tables[at + 1])


def step_kernel(
    rows_in, cols_in, spectrum, images, wide_in, cols_inv_in, twist_cols_in, twist_rows_in, out,
    led_rows, led_cols, spec, img, wide, cols_inv, twist_cols, twist_rows, grad,
    send1, recv1, send2, recv2, send3, recv3, send5, recv5,
    in_sem, known, sent, got,
):
    slab, led = lax.axis_index("slab"), lax.axis_index("led")
    core = lax.rem(slab, NC)
    z = lax.rem(lax.div(slab, NC), NZ)
    y = lax.div(slab, NC * NZ)
    yc = y * NC + core
    idle_y = jnp.where(z < NZ // 2, 0, NY - 1)
    idle = y == idle_y

    def slab_of(ny, nz, nc):
        return (ny * NZ + nz) * NC + nc

    near = [(2, 1), (2, 0), (1, 1), (3, 1), (1, 0), (3, 0), (0, 1)]
    near = [(lax.rem(y + dy, NY), lax.rem(core + dc, NC)) for dy, dc in near]
    far = [lax.rem(z + dz, NZ) for dz in FAR_FIRST]
    across = [lax.rem(led + dx, NX) for dx in (2, 1, 3)]

    loads = [
        pltpu.make_async_copy(a, b, in_sem.at[n])
        for n, (a, b) in enumerate(
            [
                (spectrum, spec),
                (rows_in, led_rows),
                (cols_in, led_cols),
                (twist_cols_in, twist_cols),
                (wide_in.at[0:2], wide.at[0:2]),
                (images, img),
                (twist_rows_in, twist_rows),
                (wide_in.at[2:12], wide.at[2:12]),
                (cols_inv_in, cols_inv),
            ]
        )
    ]
    for load in loads[:5]:
        load.start()
    barrier = pltpu.get_barrier_semaphore()

    links = [lax.rem(z + dz, NZ) for d in LINKS for dz in (d, NZ - d)]

    def greet_links(semaphore):
        for nz in links:
            pl.semaphore_signal(
                semaphore, inc=1, device_id=(slab_of(y, nz, core), led), device_id_type=MESH
            )

    greet_links(barrier)
    for ny, nc in near:
        pl.semaphore_signal(
            barrier, inc=1, device_id=(slab_of(ny, z, nc), led), device_id_type=MESH
        )
    for nx in across:
        pl.semaphore_signal(barrier, inc=1, device_id=(slab, nx), device_id_type=MESH)
    for load in loads[5:]:
        load.start()

    row_at = slab * 16 + lax.broadcasted_iota(jnp.int32, (16, 128), 0)
    lane = lax.broadcasted_iota(jnp.int32, (16, 128), 1)

    def term(offset):
        return (2 * offset + 1 - WIN) * (2 * offset + 1 - WIN)

    def inside(l, block):
        return row_terms[l] + term(lane + (block * 128 - led_cols[l])) < WIN * WIN

    def exchange(n_peers, source_of, target_of, peer_of, at):
        for n in range(n_peers):
            pltpu.make_async_remote_copy(
                src_ref=source_of(n),
                dst_ref=target_of(n),
                send_sem=sent.at[at],
                recv_sem=got.at[at],
                device_id=peer_of(n),
                device_id_type=MESH,
            ).start()

    def near_peer(n):
        ny, nc = near[n]
        return slab_of(ny, z, nc), led

    def far_peer(n):
        return slab_of(y, far[n], core), led

    def finish(semaphores, at, block):
        pltpu.make_async_copy(block, block, semaphores.at[at]).wait()

    with jax.named_scope("wait_load"):
        for load in loads[:5]:
            load.wait()
    row_terms = [term(row_at - led_rows[l]) for l in range(2)]
    pieces = []
    for l in range(2):
        values = []
        masks = [inside(l, block) for block in range(16)]
        for n1 in range(8):
            parts = []
            for part in range(2):
                first = spec[part, :, n1 * 128 : n1 * 128 + 128]
                second = spec[part, :, 1024 + n1 * 128 : 1152 + n1 * 128]
                parts.append(
                    jnp.where(masks[n1], first, 0.0) + jnp.where(masks[n1 + 8], second, 0.0)
                )
            values.append(tuple(parts))
        for k1, (re, im) in enumerate(fft(values, -1)):
            a, b = twist_cols[0, k1 : k1 + 1, :], twist_cols[1, k1 : k1 + 1, :]
            pieces.append(jnp.concatenate([re * a + im * b, im * a - re * b], axis=1))
    result = dot_left(wide, COLS_FWD, jnp.concatenate(pieces, axis=0), 1).astype(BF16)
    for l in range(2):
        send1[:, l * 32 : l * 32 + 32] = result[:, l * 128 : l * 128 + 128].reshape(8, 32, 128)
    recv1[yc] = send1[yc]
    for nc in range(NC):
        recv1[idle_y * NC + nc] = jnp.zeros_like(recv1[0])

    @pl.when(idle)
    def _():
        recv3[...] = jnp.zeros_like(recv3)

    with jax.named_scope("wait_barrier"):
        pl.semaphore_wait(barrier, len(links) + len(near) + len(across))
    greet_links(known)

    @pl.when(jnp.logical_not(idle))
    def _():
        exchange(
            len(near),
            lambda n: send1.at[near[n][0] * NC + near[n][1]],
            lambda n: recv1.at[yc],
            near_peer,
            0,
        )

    for load in loads[5:]:
        load.wait()
    moduli = []
    for l in range(2):
        stacked = jnp.concatenate(
            [img[l, :, q * 64 : q * 64 + 64] for q in range(16)], axis=0
        )
        moduli.append(jnp.sqrt(stacked).T)
    moduli = jnp.concatenate(moduli, axis=0)
    tw_re, tw_im = twist_rows[0], twist_rows[1]

    with jax.named_scope("wait_1"):

        @pl.when(jnp.logical_not(idle))
        def _():
            finish(got, 0, recv1.at[0:5])

        @pl.when(idle)
        def _():
            finish(got, 0, recv1.at[0:6])

    moved = dot(wide[FOLD], recv1[0:4].reshape(256, 128)) + dot(
        wide[FOLD + 1], recv1[4:8].reshape(256, 128)
    )
    send2[...] = moved.astype(BF16).reshape(16, 16, 128)
    recv2[z] = send2[z]
    with jax.named_scope("wait_known"):
        pl.semaphore_wait(known, len(links))
    exchange(
        len(far), lambda n: send2.at[far[n]], lambda n: recv2.at[z], far_peer, 1
    )

    with jax.named_scope("wait_2"):
        finish(got, 1, recv2.at[0:15])
    strips = recv2[...].reshape(256, 128)
    mixed = dot(wide[ROWS_FWD], strips) + dot(wide[ROWS_FWD + 1], strips)
    rows = []
    for l in range(2):
        re, im = mixed[l * 128 : l * 128 + 64], mixed[l * 128 + 64 : l * 128 + 128]
        rows.append(
            jnp.concatenate([re * tw_re + im * tw_im, im * tw_re - re * tw_im], axis=1)
        )
    field = dot_right(jnp.concatenate(rows, axis=0), wide, SHORT_FWD)
    field_re, field_im = field[:, :128], field[:, 128:]
    factor = moduli / jnp.sqrt(field_re * field_re + field_im * field_im + 0.25) - 1.0
    change = jnp.concatenate([field_re * factor, field_im * factor], axis=1)
    change = change.astype(BF16)
    back = dot(change, wide[SHORT_INV]) + dot(change, wide[SHORT_INV + 1])
    rows = []
    for l in range(2):
        re, im = back[l * 64 : l * 64 + 64, :128], back[l * 64 : l * 64 + 64, 128:]
        rows.append(re * tw_re - im * tw_im)
        rows.append(im * tw_re + re * tw_im)
    rows = jnp.concatenate(rows, axis=0).astype(BF16)
    result = dot(wide[ROWS_INV], rows) + dot(wide[ROWS_INV + 1], rows)
    send3[...] = result.astype(BF16).reshape(64, 4, 128)

    def send_back(ny, nz, nc):
        pltpu.make_async_remote_copy(
            src_ref=send3.at[(lax.rem(ny, 2) * NZ + nz) * NC + nc],
            dst_ref=recv3.at[slab],
            send_sem=sent.at[2],
            recv_sem=got.at[2],
            device_id=(slab_of(ny, nz, nc), led),
            device_id_type=MESH,
        ).start()

    for dz in FAR_FIRST + (0,):
        nz = lax.rem(z + dz, NZ)
        edge = jnp.where(nz < NZ // 2, NY - 1, 0)
        for nc in (NC - 1 - core, core):
            for ny in (edge, 1, 2):
                if dz == 0 and nc is core:
                    pl.when(y != ny)(functools.partial(send_back, ny, nz, nc))
                else:
                    send_back(ny, nz, nc)

    @pl.when(jnp.logical_not(idle))
    def _():
        recv3[slab] = send3[lax.rem(slab, 64)]

    with jax.named_scope("wait_3"):

        @pl.when(jnp.logical_not(idle))
        def _():
            finish(got, 2, recv3.at[0:127])


    home = recv3[...].reshape(512, 128)
    spread = dot(cols_inv[0], home) + dot(cols_inv[1], home)
    updates = []
    for l in range(2):
        re = spread[l * 256 : l * 256 + 128].T
        im = spread[l * 256 + 128 : l * 256 + 256].T
        values = []
        for k1 in range(8):
            a, b = twist_cols[0, k1 : k1 + 1, :], twist_cols[1, k1 : k1 + 1, :]
            kr, ki = re[k1 * 16 : k1 * 16 + 16], im[k1 * 16 : k1 * 16 + 16]
            values.append((kr * a - ki * b, ki * a + kr * b))
        updates.append(fft(values, 1))
    for block in range(16):
        masks = [inside(l, block) for l in range(2)]
        for part in range(2):
            total = jnp.where(masks[0], updates[0][block % 8][part], 0.0) + jnp.where(
                masks[1], updates[1][block % 8][part], 0.0
            )
            lanes = slice(block % 4 * 128, block % 4 * 128 + 128)
            grad[block // 4, part, :, lanes] = total
            send5[block // 4, part, :, lanes] = total.astype(BF16)
    exchange(
        len(across),
        lambda n: send5.at[across[n]],
        lambda n: recv5.at[n],
        lambda n: (slab, across[n]),
        3,
    )
    share = out.shape[2]
    total = spec[:, :, pl.ds(pl.multiple_of(led * share, share), share)] + grad[led]
    with jax.named_scope("wait_5"):
        finish(got, 3, recv5)
    for n in range(3):
        total = total + recv5[n].astype(F32)
    out[...] = total
    for at, block in ((1, send2.at[0:15]), (3, send5.at[0:3])):
        finish(sent, at, block)

    @pl.when(idle)
    def _():
        finish(sent, 2, recv3.at[0:96])

    @pl.when(jnp.logical_not(idle))
    def _():
        finish(sent, 0, send1.at[0:7])
        finish(sent, 2, recv3.at[0:95])


def body(wide, cols_inv, twist_cols, twist_rows, spectrum, led_rows, led_cols, images):
    columns = spectrum.shape[2]
    share = columns // NX
    return pl.pallas_call(
        step_kernel,
        out_shape=pltpu.VMEM((2, 16, share), F32),
        in_specs=[pl.BlockSpec(memory_space=pl.ANY)] * 8,
        out_specs=pl.BlockSpec(memory_space=pltpu.VMEM),
        scratch_shapes=[
            pltpu.SMEM((2,), jnp.int32),
            pltpu.SMEM((2,), jnp.int32),
            pltpu.VMEM((2, 16, columns), F32),
            pltpu.VMEM((2, 8, WIN), F32),
            pltpu.VMEM(wide.shape, BF16),
            pltpu.VMEM(cols_inv.shape, BF16),
            pltpu.VMEM(twist_cols.shape, F32),
            pltpu.VMEM(twist_rows.shape, F32),
            pltpu.VMEM((NX, 2, 16, share), F32),
            pltpu.VMEM((8, 64, 128), BF16),
            pltpu.VMEM((8, 64, 128), BF16),
            pltpu.VMEM((16, 16, 128), BF16),
            pltpu.VMEM((16, 16, 128), BF16),
            pltpu.VMEM((64, 4, 128), BF16),
            pltpu.VMEM((128, 4, 128), BF16),
            pltpu.VMEM((NX, 2, 16, share), BF16),
            pltpu.VMEM((3, 2, 16, share), BF16),
            pltpu.SemaphoreType.DMA((9,)),
            pltpu.SemaphoreType.REGULAR,
            pltpu.SemaphoreType.DMA((4,)),
            pltpu.SemaphoreType.DMA((4,)),
        ],
        compiler_params=pltpu.CompilerParams(collective_id=0, has_side_effects=True),
        name="ptychography_step",
    )(led_rows, led_cols, spectrum, images, wide, cols_inv, twist_cols, twist_rows)


def solution(mesh):
    tables = make_tables()
    placed = (P(None, "slab", None), P("led"), P("led"), P("led", "slab", None))
    mapped = jax.shard_map(
        body,
        mesh=mesh,
        in_specs=(P(),) * 4 + placed,
        out_specs=P(None, "slab", "led"),
        check_vma=False,
    )

    def step(spectrum, led_rows, led_cols, images):
        constants = [jnp.asarray(table) for table in tables]
        return mapped(*constants, spectrum, led_rows, led_cols, images)

    return step
```

```python
import functools

import jax
import jax.numpy as jnp
import numpy as np
from jax import lax
from jax.experimental import pallas as pl
from jax.experimental.pallas import tpu as pltpu
from jax.sharding import PartitionSpec as P

NY, NZ, NC, NX = 4, 16, 2, 4
WIN = 1024
MESH = pl.DeviceIdType.MESH
F32, BF16 = jnp.float32, jnp.bfloat16


def grid_of(*sizes):
    return np.meshgrid(*[np.arange(n) for n in sizes], indexing="ij")


def rotation(angle_index, period, out_part, in_part, sign):
    angle = 2.0 * np.pi * (angle_index % period) / period
    same = np.cos(angle)
    cross = sign * np.sin(angle)
    return np.where(out_part == in_part, same, np.where(out_part == 1, cross, -cross))


def split(table):
    high = np.asarray(table, np.float32).astype(BF16)
    low = (table - high.astype(np.float64)).astype(np.float32).astype(BF16)
    return high, low


def make_tables():
    scale = 1.0 / 32.0
    y, c, po, z, pi, n2 = grid_of(NY, NC, 2, NZ, 2, 128)
    k2 = (y * NZ + z) * NC + c
    cols_fwd = scale * rotation(k2 * n2, 128, po, pi, -1).reshape(256, 256)
    z, l, yb, c, p, y2, c2, l2, p2, z2 = grid_of(NZ, 2, 2, NC, 2, NY, NC, 2, 2, NZ)
    hit = (z == z2) & (l == l2) & (p == p2) & (c == c2) & (y2 % 2 == yb)
    fold = hit.astype(np.float64).reshape(256, 512)
    l, po, p, z, l2, yb, c, pi = grid_of(2, 2, 64, NZ, 2, 2, NC, 2)
    strip = 32 * yb + 2 * z + c
    rows_fwd = (scale * rotation(strip * p, 64, po, pi, -1) * (l == l2)).reshape(256, 256)
    strip, l, po, l2, pi, p = grid_of(64, 2, 2, 2, 2, 64)
    rows_inv = (scale * rotation(strip * p, 64, po, pi, 1) * (l == l2)).reshape(256, 256)
    pi, k1, i, po, q, k1o = grid_of(2, 8, 16, 2, 16, 8)
    short_fwd = (rotation(i * q, 16, po, pi, -1) * (k1 == k1o)).reshape(256, 256)
    pi, q, k1, po, k1o, i = grid_of(2, 16, 8, 2, 8, 16)
    short_inv = (rotation(i * q, 16, po, pi, 1) * (k1 == k1o)).reshape(256, 256)
    l, po, n2, k2, l2, pi = grid_of(2, 2, 128, 128, 2, 2)
    cols_inv = (scale * rotation(k2 * n2, 128, po, pi, 1) * (l == l2)).reshape(512, 512)
    wide = []
    for table in (cols_fwd, short_fwd, short_inv, rows_fwd, rows_inv):
        wide.extend(split(table))
    for table in (fold[:, :256], fold[:, 256:]):
        wide.append(np.asarray(table, np.float32).astype(BF16))
    k1, n2 = grid_of(8, 128)
    angle = 2.0 * np.pi * ((k1 * n2) % WIN) / WIN
    twist_cols = np.stack([np.cos(angle), np.sin(angle)]).astype(np.float32)
    p, k1, i = grid_of(64, 8, 16)
    angle = (2.0 * np.pi * ((p * i) % WIN) / WIN).reshape(64, 128)
    twist_rows = np.stack([np.cos(angle), np.sin(angle)]).astype(np.float32)
    return np.stack(wide), split(cols_inv)[0], twist_cols, twist_rows


COLS_FWD, SHORT_FWD, SHORT_INV, ROWS_FWD, ROWS_INV, FOLD = range(0, 12, 2)
LINKS = (1, 3, 4)
FAR_FIRST = (8, 7, 9, 6, 10, 5, 11, 4, 12, 3, 13, 2, 14, 1, 15)


def fft(values, sign):
    size = len(values)
    if size == 1:
        return values
    even, odd = fft(values[0::2], sign), fft(values[1::2], sign)
    low, high = [], []
    for k in range(size // 2):
        (er, ei), (re, im) = even[k], odd[k]
        if k == 0:
            tr, ti = re, im
        elif 4 * k == size:
            tr, ti = (-im, re) if sign > 0 else (im, -re)
        else:
            a = float(np.cos(2 * np.pi * k / size))
            b = float(np.sin(2 * np.pi * k / size)) * sign
            tr, ti = a * re - b * im, a * im + b * re
        low.append((er + tr, ei + ti))
        high.append((er - tr, ei - ti))
    return low + high


def halves(value):
    high = value.astype(BF16)
    return high, (value - high.astype(F32)).astype(BF16)


def dot(left, right, right_dim=0):
    return lax.dot_general(
        left, right, (((1,), (right_dim,)), ((), ())), preferred_element_type=F32
    )


def dot_left(tables, at, value, right_dim=0):
    high, low = halves(value)
    return (
        dot(tables[at], high, right_dim)
        + dot(tables[at + 1], high, right_dim)
        + dot(tables[at], low, right_dim)
    )


def step_kernel(
    rows_in, cols_in, spectrum, images, wide_in, cols_inv_in, twist_cols_in, twist_rows_in, out,
    led_rows, led_cols, spec, img, wide, cols_inv, twist_cols, twist_rows, grad,
    send1, recv1, send2, recv2, send3, recv3, send5, recv5,
    in_sem, known, sent, got,
):
    slab, led = lax.axis_index("slab"), lax.axis_index("led")
    core = lax.rem(slab, NC)
    z = lax.rem(lax.div(slab, NC), NZ)
    y = lax.div(slab, NC * NZ)
    yc = y * NC + core
    idle_y = jnp.where(z < NZ // 2, 0, NY - 1)
    idle = y == idle_y

    def slab_of(ny, nz, nc):
        return (ny * NZ + nz) * NC + nc

    near = [(2, 1), (2, 0), (1, 1), (3, 1), (1, 0), (3, 0), (0, 1)]
    near = [(lax.rem(y + dy, NY), lax.rem(core + dc, NC)) for dy, dc in near]
    far = [lax.rem(z + dz, NZ) for dz in FAR_FIRST]
    across = [lax.rem(led + dx, NX) for dx in (2, 1, 3)]

    loads = [
        pltpu.make_async_copy(a, b, in_sem.at[n])
        for n, (a, b) in enumerate(
            [
                (spectrum, spec),
                (rows_in, led_rows),
                (cols_in, led_cols),
                (twist_cols_in, twist_cols),
                (wide_in.at[0:2], wide.at[0:2]),
                (images, img),
                (twist_rows_in, twist_rows),
                (wide_in.at[2:12], wide.at[2:12]),
                (cols_inv_in, cols_inv),
            ]
        )
    ]
    barrier = pltpu.get_barrier_semaphore()

    links = [lax.rem(z + dz, NZ) for d in LINKS for dz in (d, NZ - d)]

    def greet_links(semaphore):
        for nz in links:
            pl.semaphore_signal(
                semaphore, inc=1, device_id=(slab_of(y, nz, core), led), device_id_type=MESH
            )

    greet_links(barrier)
    for ny, nc in near:
        pl.semaphore_signal(
            barrier, inc=1, device_id=(slab_of(ny, z, nc), led), device_id_type=MESH
        )
    for nx in across:
        pl.semaphore_signal(barrier, inc=1, device_id=(slab, nx), device_id_type=MESH)
    for load in loads:
        load.start()

    row_at = slab * 16 + lax.broadcasted_iota(jnp.int32, (16, 128), 0)
    lane = lax.broadcasted_iota(jnp.int32, (16, 128), 1)

    def term(offset):
        return (2 * offset + 1 - WIN) * (2 * offset + 1 - WIN)

    def inside(l, block):
        return row_terms[l] + term(lane + (block * 128 - led_cols[l])) < WIN * WIN

    def exchange(n_peers, source_of, target_of, peer_of, at):
        for n in range(n_peers):
            pltpu.make_async_remote_copy(
                src_ref=source_of(n),
                dst_ref=target_of(n),
                send_sem=sent.at[at],
                recv_sem=got.at[at],
                device_id=peer_of(n),
                device_id_type=MESH,
            ).start()

    def near_peer(n):
        ny, nc = near[n]
        return slab_of(ny, z, nc), led

    def far_peer(n):
        return slab_of(y, far[n], core), led

    def finish(semaphores, at, block):
        pltpu.make_async_copy(block, block, semaphores.at[at]).wait()

    with jax.named_scope("wait_load"):
        for load in loads[:5]:
            load.wait()
    row_terms = [term(row_at - led_rows[l]) for l in range(2)]
    pieces = []
    for l in range(2):
        values = []
        masks = [inside(l, block) for block in range(16)]
        for n1 in range(8):
            parts = []
            for part in range(2):
                first = spec[part, :, n1 * 128 : n1 * 128 + 128]
                second = spec[part, :, 1024 + n1 * 128 : 1152 + n1 * 128]
                parts.append(
                    jnp.where(masks[n1], first, 0.0) + jnp.where(masks[n1 + 8], second, 0.0)
                )
            values.append(tuple(parts))
        for k1, (re, im) in enumerate(fft(values, -1)):
            a, b = twist_cols[0, k1 : k1 + 1, :], twist_cols[1, k1 : k1 + 1, :]
            pieces.append(jnp.concatenate([re * a + im * b, im * a - re * b], axis=1))
    result = dot_left(wide, COLS_FWD, jnp.concatenate(pieces, axis=0), 1).astype(BF16)
    for l in range(2):
        send1[:, l * 32 : l * 32 + 32] = result[:, l * 128 : l * 128 + 128].reshape(8, 32, 128)
    recv1[yc] = send1[yc]
    for nc in range(NC):
        recv1[idle_y * NC + nc] = jnp.zeros_like(recv1[0])

    @pl.when(idle)
    def _():
        recv3[...] = jnp.zeros_like(recv3)

    with jax.named_scope("wait_barrier"):
        pl.semaphore_wait(barrier, len(links) + len(near) + len(across))
    greet_links(known)

    @pl.when(jnp.logical_not(idle))
    def _():
        exchange(
            len(near),
            lambda n: send1.at[near[n][0] * NC + near[n][1]],
            lambda n: recv1.at[yc],
            near_peer,
            0,
        )

    for load in loads[5:]:
        load.wait()
    moduli = []
    for l in range(2):
        stacked = jnp.concatenate(
            [img[l, :, q * 64 : q * 64 + 64] for q in range(16)], axis=0
        )
        moduli.append(jnp.sqrt(stacked).T)
    moduli = jnp.concatenate(moduli, axis=0)
    tw_re, tw_im = twist_rows[0], twist_rows[1]

    with jax.named_scope("wait_1"):

        @pl.when(jnp.logical_not(idle))
        def _():
            finish(got, 0, recv1.at[0:5])

        @pl.when(idle)
        def _():
            finish(got, 0, recv1.at[0:6])

    moved = dot(wide[FOLD], recv1[0:4].reshape(256, 128)) + dot(
        wide[FOLD + 1], recv1[4:8].reshape(256, 128)
    )
    send2[...] = moved.astype(BF16).reshape(16, 16, 128)
    recv2[z] = send2[z]
    with jax.named_scope("wait_known"):
        pl.semaphore_wait(known, len(links))
    exchange(
        len(far), lambda n: send2.at[far[n]], lambda n: recv2.at[z], far_peer, 1
    )

    with jax.named_scope("wait_2"):
        finish(got, 1, recv2.at[0:15])
    strips = recv2[...].reshape(256, 128)
    mixed = dot(wide[ROWS_FWD], strips) + dot(wide[ROWS_FWD + 1], strips)
    rows = []
    for l in range(2):
        re, im = mixed[l * 128 : l * 128 + 64], mixed[l * 128 + 64 : l * 128 + 128]
        rows.append(
            jnp.concatenate([re * tw_re + im * tw_im, im * tw_re - re * tw_im], axis=1)
        )
    rows = jnp.concatenate(rows, axis=0).astype(BF16)
    field = dot(rows, wide[SHORT_FWD]) + dot(rows, wide[SHORT_FWD + 1])
    field_re, field_im = field[:, :128], field[:, 128:]
    factor = moduli / jnp.sqrt(field_re * field_re + field_im * field_im + 0.25) - 1.0
    change = jnp.concatenate([field_re * factor, field_im * factor], axis=1)
    change = change.astype(BF16)
    back = dot(change, wide[SHORT_INV]) + dot(change, wide[SHORT_INV + 1])
    rows = []
    for l in range(2):
        re, im = back[l * 64 : l * 64 + 64, :128], back[l * 64 : l * 64 + 64, 128:]
        rows.append(re * tw_re - im * tw_im)
        rows.append(im * tw_re + re * tw_im)
    rows = jnp.concatenate(rows, axis=0).astype(BF16)
    result = dot(wide[ROWS_INV], rows) + dot(wide[ROWS_INV + 1], rows)
    send3[...] = result.astype(BF16).reshape(64, 4, 128)

    def send_back(ny, nz, nc):
        pltpu.make_async_remote_copy(
            src_ref=send3.at[(lax.rem(ny, 2) * NZ + nz) * NC + nc],
            dst_ref=recv3.at[slab],
            send_sem=sent.at[2],
            recv_sem=got.at[2],
            device_id=(slab_of(ny, nz, nc), led),
            device_id_type=MESH,
        ).start()

    for dz in FAR_FIRST + (0,):
        nz = lax.rem(z + dz, NZ)
        edge = jnp.where(nz < NZ // 2, NY - 1, 0)
        for nc in (NC - 1 - core, core):
            for ny in (edge, 1, 2):
                if dz == 0 and nc is core:
                    pl.when(y != ny)(functools.partial(send_back, ny, nz, nc))
                else:
                    send_back(ny, nz, nc)

    @pl.when(jnp.logical_not(idle))
    def _():
        recv3[slab] = send3[lax.rem(slab, 64)]

    with jax.named_scope("wait_3"):

        @pl.when(jnp.logical_not(idle))
        def _():
            finish(got, 2, recv3.at[0:127])


    home = recv3[...].reshape(512, 128)
    spread = dot(cols_inv[...], home)
    updates = []
    for l in range(2):
        re = spread[l * 256 : l * 256 + 128].T
        im = spread[l * 256 + 128 : l * 256 + 256].T
        values = []
        for k1 in range(8):
            a, b = twist_cols[0, k1 : k1 + 1, :], twist_cols[1, k1 : k1 + 1, :]
            kr, ki = re[k1 * 16 : k1 * 16 + 16], im[k1 * 16 : k1 * 16 + 16]
            values.append((kr * a - ki * b, ki * a + kr * b))
        updates.append(fft(values, 1))
    for block in range(16):
        masks = [inside(l, block) for l in range(2)]
        for part in range(2):
            total = jnp.where(masks[0], updates[0][block % 8][part], 0.0) + jnp.where(
                masks[1], updates[1][block % 8][part], 0.0
            )
            lanes = slice(block % 4 * 128, block % 4 * 128 + 128)
            grad[block // 4, part, :, lanes] = total
            send5[block // 4, part, :, lanes] = total.astype(BF16)
    exchange(
        len(across),
        lambda n: send5.at[across[n]],
        lambda n: recv5.at[n],
        lambda n: (slab, across[n]),
        3,
    )
    share = out.shape[2]
    total = spec[:, :, pl.ds(pl.multiple_of(led * share, share), share)] + grad[led]
    with jax.named_scope("wait_5"):
        finish(got, 3, recv5)
    for n in range(3):
        total = total + recv5[n].astype(F32)
    out[...] = total
    for at, block in ((1, send2.at[0:15]), (3, send5.at[0:3])):
        finish(sent, at, block)

    @pl.when(idle)
    def _():
        finish(sent, 2, recv3.at[0:96])

    @pl.when(jnp.logical_not(idle))
    def _():
        finish(sent, 0, send1.at[0:7])
        finish(sent, 2, recv3.at[0:95])


def body(wide, cols_inv, twist_cols, twist_rows, spectrum, led_rows, led_cols, images):
    columns = spectrum.shape[2]
    share = columns // NX
    return pl.pallas_call(
        step_kernel,
        out_shape=pltpu.VMEM((2, 16, share), F32),
        in_specs=[pl.BlockSpec(memory_space=pl.ANY)] * 8,
        out_specs=pl.BlockSpec(memory_space=pltpu.VMEM),
        scratch_shapes=[
            pltpu.SMEM((2,), jnp.int32),
            pltpu.SMEM((2,), jnp.int32),
            pltpu.VMEM((2, 16, columns), F32),
            pltpu.VMEM((2, 8, WIN), F32),
            pltpu.VMEM(wide.shape, BF16),
            pltpu.VMEM(cols_inv.shape, BF16),
            pltpu.VMEM(twist_cols.shape, F32),
            pltpu.VMEM(twist_rows.shape, F32),
            pltpu.VMEM((NX, 2, 16, share), F32),
            pltpu.VMEM((8, 64, 128), BF16),
            pltpu.VMEM((8, 64, 128), BF16),
            pltpu.VMEM((16, 16, 128), BF16),
            pltpu.VMEM((16, 16, 128), BF16),
            pltpu.VMEM((64, 4, 128), BF16),
            pltpu.VMEM((128, 4, 128), BF16),
            pltpu.VMEM((NX, 2, 16, share), BF16),
            pltpu.VMEM((3, 2, 16, share), BF16),
            pltpu.SemaphoreType.DMA((9,)),
            pltpu.SemaphoreType.REGULAR,
            pltpu.SemaphoreType.DMA((4,)),
            pltpu.SemaphoreType.DMA((4,)),
        ],
        compiler_params=pltpu.CompilerParams(collective_id=0, has_side_effects=True),
        name="ptychography_step",
    )(led_rows, led_cols, spectrum, images, wide, cols_inv, twist_cols, twist_rows)


def solution(mesh):
    tables = make_tables()
    placed = (P(None, "slab", None), P("led"), P("led"), P("led", "slab", None))
    mapped = jax.shard_map(
        body,
        mesh=mesh,
        in_specs=(P(),) * 4 + placed,
        out_specs=P(None, "slab", "led"),
        check_vma=False,
    )

    def step(spectrum, led_rows, led_cols, images):
        constants = [jnp.asarray(table) for table in tables]
        return mapped(*constants, spectrum, led_rows, led_cols, images)

    return step
```

```python
import functools

import jax
import jax.numpy as jnp
import numpy as np
from jax import lax
from jax.experimental import pallas as pl
from jax.experimental.pallas import tpu as pltpu
from jax.sharding import PartitionSpec as P

NY, NZ, NC, NX = 4, 16, 2, 4
WIN = 1024
MESH = pl.DeviceIdType.MESH
F32, BF16 = jnp.float32, jnp.bfloat16


def grid_of(*sizes):
    return np.meshgrid(*[np.arange(n) for n in sizes], indexing="ij")


def rotation(angle_index, period, out_part, in_part, sign):
    angle = 2.0 * np.pi * (angle_index % period) / period
    same = np.cos(angle)
    cross = sign * np.sin(angle)
    return np.where(out_part == in_part, same, np.where(out_part == 1, cross, -cross))


def split(table):
    high = np.asarray(table, np.float32).astype(BF16)
    low = (table - high.astype(np.float64)).astype(np.float32).astype(BF16)
    return high, low


def make_tables():
    scale = 1.0 / 32.0
    y, c, z, po, pi, n2 = grid_of(NY, NC, NZ, 2, 2, 128)
    k2 = (y * NZ + z) * NC + c
    cols_fwd = scale * rotation(k2 * n2, 128, po, pi, -1).reshape(256, 256)
    l, po, p, yb, c, l2, z, pi = grid_of(2, 2, 64, 2, NC, 2, NZ, 2)
    strip = 32 * yb + 2 * z + c
    rows_fwd = (scale * rotation(strip * p, 64, po, pi, -1) * (l == l2)).reshape(256, 256)
    strip, l, po, l2, pi, p = grid_of(64, 2, 2, 2, 2, 64)
    rows_inv = (scale * rotation(strip * p, 64, po, pi, 1) * (l == l2)).reshape(256, 256)
    pi, k1, i, po, q, k1o = grid_of(2, 8, 16, 2, 16, 8)
    short_fwd = (rotation(i * q, 16, po, pi, -1) * (k1 == k1o)).reshape(256, 256)
    pi, q, k1, po, k1o, i = grid_of(2, 16, 8, 2, 8, 16)
    short_inv = (rotation(i * q, 16, po, pi, 1) * (k1 == k1o)).reshape(256, 256)
    l, po, n2, k2, l2, pi = grid_of(2, 2, 128, 128, 2, 2)
    cols_inv = (scale * rotation(k2 * n2, 128, po, pi, 1) * (l == l2)).reshape(512, 512)
    wide = []
    for table in (cols_fwd, short_fwd, short_inv, rows_fwd, rows_inv):
        wide.extend(split(table))
    k1, n2 = grid_of(8, 128)
    angle = 2.0 * np.pi * ((k1 * n2) % WIN) / WIN
    twist_cols = np.stack([np.cos(angle), np.sin(angle)]).astype(np.float32)
    p, k1, i = grid_of(64, 8, 16)
    angle = (2.0 * np.pi * ((p * i) % WIN) / WIN).reshape(64, 128)
    twist_rows = np.stack([np.cos(angle), np.sin(angle)]).astype(np.float32)
    return np.stack(wide), split(cols_inv)[0], twist_cols, twist_rows


COLS_FWD, SHORT_FWD, SHORT_INV, ROWS_FWD, ROWS_INV = range(0, 10, 2)
LINKS = (1, 3, 4)
FAR_FIRST = (8, 7, 9, 6, 10, 5, 11, 4, 12, 3, 13, 2, 14, 1, 15)


def fft(values, sign):
    size = len(values)
    if size == 1:
        return values
    even, odd = fft(values[0::2], sign), fft(values[1::2], sign)
    low, high = [], []
    for k in range(size // 2):
        (er, ei), (re, im) = even[k], odd[k]
        if k == 0:
            tr, ti = re, im
        elif 4 * k == size:
            tr, ti = (-im, re) if sign > 0 else (im, -re)
        else:
            a = float(np.cos(2 * np.pi * k / size))
            b = float(np.sin(2 * np.pi * k / size)) * sign
            tr, ti = a * re - b * im, a * im + b * re
        low.append((er + tr, ei + ti))
        high.append((er - tr, ei - ti))
    return low + high


def halves(value):
    high = value.astype(BF16)
    return high, (value - high.astype(F32)).astype(BF16)


def dot(left, right, right_dim=0):
    return lax.dot_general(
        left, right, (((1,), (right_dim,)), ((), ())), preferred_element_type=F32
    )


def dot_left(tables, at, value, right_dim=0):
    high, low = halves(value)
    return (
        dot(tables[at], high, right_dim)
        + dot(tables[at + 1], high, right_dim)
        + dot(tables[at], low, right_dim)
    )


def step_kernel(
    rows_in, cols_in, spectrum, images, wide_in, cols_inv_in, twist_cols_in, twist_rows_in, out,
    led_rows, led_cols, spec, img, wide, cols_inv, twist_cols, twist_rows, grad,
    send1, recv1, send2, recv2, send3, recv3, send5, recv5,
    in_sem, known, sent, got,
):
    slab, led = lax.axis_index("slab"), lax.axis_index("led")
    core = lax.rem(slab, NC)
    z = lax.rem(lax.div(slab, NC), NZ)
    y = lax.div(slab, NC * NZ)
    yc = y * NC + core
    idle_y = jnp.where(z < NZ // 2, 0, NY - 1)
    idle = y == idle_y

    def slab_of(ny, nz, nc):
        return (ny * NZ + nz) * NC + nc

    near = [(2, 1), (2, 0), (1, 1), (3, 1), (1, 0), (3, 0), (0, 1)]
    near = [(lax.rem(y + dy, NY), lax.rem(core + dc, NC)) for dy, dc in near]
    far = [lax.rem(z + dz, NZ) for dz in FAR_FIRST]
    across = [lax.rem(led + dx, NX) for dx in (2, 1, 3)]

    loads = [
        pltpu.make_async_copy(a, b, in_sem.at[n])
        for n, (a, b) in enumerate(
            [
                (spectrum, spec),
                (rows_in, led_rows),
                (cols_in, led_cols),
                (twist_cols_in, twist_cols),
                (wide_in.at[0:2], wide.at[0:2]),
                (images, img),
                (twist_rows_in, twist_rows),
                (wide_in.at[2:10], wide.at[2:10]),
                (cols_inv_in, cols_inv),
            ]
        )
    ]
    barrier = pltpu.get_barrier_semaphore()

    links = [lax.rem(z + dz, NZ) for d in LINKS for dz in (d, NZ - d)]

    def greet_links(semaphore):
        for nz in links:
            pl.semaphore_signal(
                semaphore, inc=1, device_id=(slab_of(y, nz, core), led), device_id_type=MESH
            )

    greet_links(barrier)
    for ny, nc in near:
        pl.semaphore_signal(
            barrier, inc=1, device_id=(slab_of(ny, z, nc), led), device_id_type=MESH
        )
    for nx in across:
        pl.semaphore_signal(barrier, inc=1, device_id=(slab, nx), device_id_type=MESH)
    for load in loads:
        load.start()

    row_at = slab * 16 + lax.broadcasted_iota(jnp.int32, (16, 128), 0)
    lane = lax.broadcasted_iota(jnp.int32, (16, 128), 1)

    def term(offset):
        return (2 * offset + 1 - WIN) * (2 * offset + 1 - WIN)

    def inside(l, block):
        return row_terms[l] + term(lane + (block * 128 - led_cols[l])) < WIN * WIN

    def exchange(n_peers, source_of, target_of, peer_of, at):
        for n in range(n_peers):
            pltpu.make_async_remote_copy(
                src_ref=source_of(n),
                dst_ref=target_of(n),
                send_sem=sent.at[at],
                recv_sem=got.at[at],
                device_id=peer_of(n),
                device_id_type=MESH,
            ).start()

    def near_peer(n):
        ny, nc = near[n]
        return slab_of(ny, z, nc), led

    def far_peer(n):
        return slab_of(y, far[n], core), led

    def finish(semaphores, at, block):
        pltpu.make_async_copy(block, block, semaphores.at[at]).wait()

    with jax.named_scope("wait_load"):
        for load in loads[:5]:
            load.wait()
    row_terms = [term(row_at - led_rows[l]) for l in range(2)]
    pieces = []
    for l in range(2):
        values = []
        masks = [inside(l, block) for block in range(16)]
        for n1 in range(8):
            parts = []
            for part in range(2):
                first = spec[part, :, n1 * 128 : n1 * 128 + 128]
                second = spec[part, :, 1024 + n1 * 128 : 1152 + n1 * 128]
                parts.append(
                    jnp.where(masks[n1], first, 0.0) + jnp.where(masks[n1 + 8], second, 0.0)
                )
            values.append(tuple(parts))
        for k1, (re, im) in enumerate(fft(values, -1)):
            a, b = twist_cols[0, k1 : k1 + 1, :], twist_cols[1, k1 : k1 + 1, :]
            pieces.append(jnp.concatenate([re * a + im * b, im * a - re * b], axis=1))
    result = dot_left(wide, COLS_FWD, jnp.concatenate(pieces, axis=0), 1).astype(BF16)
    for l in range(2):
        send1[:, l] = result[:, l * 128 : l * 128 + 128].reshape(8, NZ, 2, 128)
    recv1[yc] = send1[yc]
    for nc in range(NC):
        recv1[idle_y * NC + nc] = jnp.zeros_like(recv1[0])

    @pl.when(idle)
    def _():
        recv3[...] = jnp.zeros_like(recv3)

    with jax.named_scope("wait_barrier"):
        pl.semaphore_wait(barrier, len(links) + len(near) + len(across))
    greet_links(known)

    @pl.when(jnp.logical_not(idle))
    def _():
        exchange(
            len(near),
            lambda n: send1.at[near[n][0] * NC + near[n][1]],
            lambda n: recv1.at[yc],
            near_peer,
            0,
        )

    for load in loads[5:]:
        load.wait()
    moduli = []
    for l in range(2):
        stacked = jnp.concatenate(
            [img[l, :, q * 64 : q * 64 + 64] for q in range(16)], axis=0
        )
        moduli.append(jnp.sqrt(stacked).T)
    moduli = jnp.concatenate(moduli, axis=0)
    tw_re, tw_im = twist_rows[0], twist_rows[1]

    with jax.named_scope("wait_1"):

        @pl.when(jnp.logical_not(idle))
        def _():
            finish(got, 0, recv1.at[0:5])

        @pl.when(idle)
        def _():
            finish(got, 0, recv1.at[0:6])

    send2[...] = recv1[0:4] + recv1[4:8]
    recv2[:, :, z] = send2[:, :, z]
    with jax.named_scope("wait_known"):
        pl.semaphore_wait(known, len(links))
    exchange(
        len(far), lambda n: send2.at[:, :, far[n]], lambda n: recv2.at[:, :, z], far_peer, 1
    )

    with jax.named_scope("wait_2"):
        finish(got, 1, recv2.at[:, :, 0:15])
    strips = recv2[...].reshape(256, 128)
    mixed = dot(wide[ROWS_FWD], strips) + dot(wide[ROWS_FWD + 1], strips)
    rows = []
    for l in range(2):
        re, im = mixed[l * 128 : l * 128 + 64], mixed[l * 128 + 64 : l * 128 + 128]
        rows.append(
            jnp.concatenate([re * tw_re + im * tw_im, im * tw_re - re * tw_im], axis=1)
        )
    rows = jnp.concatenate(rows, axis=0).astype(BF16)
    field = dot(rows, wide[SHORT_FWD]) + dot(rows, wide[SHORT_FWD + 1])
    field_re, field_im = field[:, :128], field[:, 128:]
    factor = moduli / jnp.sqrt(field_re * field_re + field_im * field_im + 0.25) - 1.0
    change = jnp.concatenate([field_re * factor, field_im * factor], axis=1)
    change = change.astype(BF16)
    back = dot(change, wide[SHORT_INV]) + dot(change, wide[SHORT_INV + 1])
    rows = []
    for l in range(2):
        re, im = back[l * 64 : l * 64 + 64, :128], back[l * 64 : l * 64 + 64, 128:]
        rows.append(re * tw_re - im * tw_im)
        rows.append(im * tw_re + re * tw_im)
    rows = jnp.concatenate(rows, axis=0).astype(BF16)
    result = dot(wide[ROWS_INV], rows) + dot(wide[ROWS_INV + 1], rows)
    send3[...] = result.astype(BF16).reshape(64, 4, 128)

    def send_back(ny, nz, nc):
        pltpu.make_async_remote_copy(
            src_ref=send3.at[(lax.rem(ny, 2) * NZ + nz) * NC + nc],
            dst_ref=recv3.at[slab],
            send_sem=sent.at[2],
            recv_sem=got.at[2],
            device_id=(slab_of(ny, nz, nc), led),
            device_id_type=MESH,
        ).start()

    for dz in FAR_FIRST + (0,):
        nz = lax.rem(z + dz, NZ)
        edge = jnp.where(nz < NZ // 2, NY - 1, 0)
        for nc in (NC - 1 - core, core):
            for ny in (edge, 1, 2):
                if dz == 0 and nc is core:
                    pl.when(y != ny)(functools.partial(send_back, ny, nz, nc))
                else:
                    send_back(ny, nz, nc)

    @pl.when(jnp.logical_not(idle))
    def _():
        recv3[slab] = send3[lax.rem(slab, 64)]

    with jax.named_scope("wait_3"):

        @pl.when(jnp.logical_not(idle))
        def _():
            finish(got, 2, recv3.at[0:127])


    home = recv3[...].reshape(512, 128)
    spread = dot(cols_inv[...], home)
    updates = []
    for l in range(2):
        re = spread[l * 256 : l * 256 + 128].T
        im = spread[l * 256 + 128 : l * 256 + 256].T
        values = []
        for k1 in range(8):
            a, b = twist_cols[0, k1 : k1 + 1, :], twist_cols[1, k1 : k1 + 1, :]
            kr, ki = re[k1 * 16 : k1 * 16 + 16], im[k1 * 16 : k1 * 16 + 16]
            values.append((kr * a - ki * b, ki * a + kr * b))
        updates.append(fft(values, 1))
    for block in range(16):
        masks = [inside(l, block) for l in range(2)]
        for part in range(2):
            total = jnp.where(masks[0], updates[0][block % 8][part], 0.0) + jnp.where(
                masks[1], updates[1][block % 8][part], 0.0
            )
            lanes = slice(block % 4 * 128, block % 4 * 128 + 128)
            grad[block // 4, part, :, lanes] = total
            send5[block // 4, part, :, lanes] = total.astype(BF16)
    exchange(
        len(across),
        lambda n: send5.at[across[n]],
        lambda n: recv5.at[n],
        lambda n: (slab, across[n]),
        3,
    )
    share = out.shape[2]
    total = spec[:, :, pl.ds(pl.multiple_of(led * share, share), share)] + grad[led]
    with jax.named_scope("wait_5"):
        finish(got, 3, recv5)
    for n in range(3):
        total = total + recv5[n].astype(F32)
    out[...] = total
    for at, block in ((1, send2.at[:, :, 0:15]), (3, send5.at[0:3])):
        finish(sent, at, block)

    @pl.when(idle)
    def _():
        finish(sent, 2, recv3.at[0:96])

    @pl.when(jnp.logical_not(idle))
    def _():
        finish(sent, 0, send1.at[0:7])
        finish(sent, 2, recv3.at[0:95])


def body(wide, cols_inv, twist_cols, twist_rows, spectrum, led_rows, led_cols, images):
    columns = spectrum.shape[2]
    share = columns // NX
    return pl.pallas_call(
        step_kernel,
        out_shape=pltpu.VMEM((2, 16, share), F32),
        in_specs=[pl.BlockSpec(memory_space=pl.ANY)] * 8,
        out_specs=pl.BlockSpec(memory_space=pltpu.VMEM),
        scratch_shapes=[
            pltpu.SMEM((2,), jnp.int32),
            pltpu.SMEM((2,), jnp.int32),
            pltpu.VMEM((2, 16, columns), F32),
            pltpu.VMEM((2, 8, WIN), F32),
            pltpu.VMEM(wide.shape, BF16),
            pltpu.VMEM(cols_inv.shape, BF16),
            pltpu.VMEM(twist_cols.shape, F32),
            pltpu.VMEM(twist_rows.shape, F32),
            pltpu.VMEM((NX, 2, 16, share), F32),
            pltpu.VMEM((8, 2, NZ, 2, 128), BF16),
            pltpu.VMEM((8, 2, NZ, 2, 128), BF16),
            pltpu.VMEM((4, 2, NZ, 2, 128), BF16),
            pltpu.VMEM((4, 2, NZ, 2, 128), BF16),
            pltpu.VMEM((64, 4, 128), BF16),
            pltpu.VMEM((128, 4, 128), BF16),
            pltpu.VMEM((NX, 2, 16, share), BF16),
            pltpu.VMEM((3, 2, 16, share), BF16),
            pltpu.SemaphoreType.DMA((9,)),
            pltpu.SemaphoreType.REGULAR,
            pltpu.SemaphoreType.DMA((4,)),
            pltpu.SemaphoreType.DMA((4,)),
        ],
        compiler_params=pltpu.CompilerParams(collective_id=0, has_side_effects=True),
        name="ptychography_step",
    )(led_rows, led_cols, spectrum, images, wide, cols_inv, twist_cols, twist_rows)


def solution(mesh):
    tables = make_tables()
    placed = (P(None, "slab", None), P("led"), P("led"), P("led", "slab", None))
    mapped = jax.shard_map(
        body,
        mesh=mesh,
        in_specs=(P(),) * 4 + placed,
        out_specs=P(None, "slab", "led"),
        check_vma=False,
    )

    def step(spectrum, led_rows, led_cols, images):
        constants = [jnp.asarray(table) for table in tables]
        return mapped(*constants, spectrum, led_rows, led_cols, images)

    return step
```

```python
import functools

import jax
import jax.numpy as jnp
import numpy as np
from jax import lax
from jax.experimental import pallas as pl
from jax.experimental.pallas import tpu as pltpu
from jax.sharding import PartitionSpec as P

NY, NZ, NC, NX = 4, 16, 2, 4
WIN = 1024
MESH = pl.DeviceIdType.MESH
F32, BF16 = jnp.float32, jnp.bfloat16


def grid_of(*sizes):
    return np.meshgrid(*[np.arange(n) for n in sizes], indexing="ij")


def rotation(angle_index, period, out_part, in_part, sign):
    angle = 2.0 * np.pi * (angle_index % period) / period
    same = np.cos(angle)
    cross = sign * np.sin(angle)
    return np.where(out_part == in_part, same, np.where(out_part == 1, cross, -cross))


def split(table):
    high = np.asarray(table, np.float32).astype(BF16)
    low = (table - high.astype(np.float64)).astype(np.float32).astype(BF16)
    return high, low


def make_tables():
    scale = 1.0 / 32.0
    y, c, z, po, pi, n2 = grid_of(NY, NC, NZ, 2, 2, 128)
    k2 = (y * NZ + z) * NC + c
    cols_fwd = scale * rotation(k2 * n2, 128, po, pi, -1).reshape(256, 256)
    l, po, p, yb, c, l2, z, pi = grid_of(2, 2, 64, 2, NC, 2, NZ, 2)
    strip = 32 * yb + 2 * z + c
    rows_fwd = (scale * rotation(strip * p, 64, po, pi, -1) * (l == l2)).reshape(256, 256)
    strip, l, po, l2, pi, p = grid_of(64, 2, 2, 2, 2, 64)
    rows_inv = (scale * rotation(strip * p, 64, po, pi, 1) * (l == l2)).reshape(256, 256)
    pi, k1, i, po, q, k1o = grid_of(2, 8, 16, 2, 16, 8)
    short_fwd = (rotation(i * q, 16, po, pi, -1) * (k1 == k1o)).reshape(256, 256)
    pi, q, k1, po, k1o, i = grid_of(2, 16, 8, 2, 8, 16)
    short_inv = (rotation(i * q, 16, po, pi, 1) * (k1 == k1o)).reshape(256, 256)
    l, po, n2, k2, l2, pi = grid_of(2, 2, 128, 128, 2, 2)
    cols_inv = (scale * rotation(k2 * n2, 128, po, pi, 1) * (l == l2)).reshape(512, 512)
    wide = []
    for table in (cols_fwd, short_fwd, short_inv, rows_fwd, rows_inv):
        wide.extend(split(table))
    k1, n2 = grid_of(8, 128)
    angle = 2.0 * np.pi * ((k1 * n2) % WIN) / WIN
    twist_cols = np.stack([np.cos(angle), np.sin(angle)]).astype(np.float32)
    p, k1, i = grid_of(64, 8, 16)
    angle = (2.0 * np.pi * ((p * i) % WIN) / WIN).reshape(64, 128)
    twist_rows = np.stack([np.cos(angle), np.sin(angle)]).astype(np.float32)
    return np.stack(wide), split(cols_inv)[0], twist_cols, twist_rows


COLS_FWD, SHORT_FWD, SHORT_INV, ROWS_FWD, ROWS_INV = range(0, 10, 2)
LINKS = (1, 3, 4)
FAR_FIRST = (8, 7, 9, 6, 10, 5, 11, 4, 12, 3, 13, 2, 14, 1, 15)


def fft(values, sign):
    size = len(values)
    if size == 1:
        return values
    even, odd = fft(values[0::2], sign), fft(values[1::2], sign)
    low, high = [], []
    for k in range(size // 2):
        (er, ei), (re, im) = even[k], odd[k]
        if k == 0:
            tr, ti = re, im
        elif 4 * k == size:
            tr, ti = (-im, re) if sign > 0 else (im, -re)
        else:
            a = float(np.cos(2 * np.pi * k / size))
            b = float(np.sin(2 * np.pi * k / size)) * sign
            tr, ti = a * re - b * im, a * im + b * re
        low.append((er + tr, ei + ti))
        high.append((er - tr, ei - ti))
    return low + high


def halves(value):
    high = value.astype(BF16)
    return high, (value - high.astype(F32)).astype(BF16)


def dot(left, right, right_dim=0):
    return lax.dot_general(
        left, right, (((1,), (right_dim,)), ((), ())), preferred_element_type=F32
    )


def dot_left(tables, at, value, right_dim=0):
    high, low = halves(value)
    return (
        dot(tables[at], high, right_dim)
        + dot(tables[at + 1], high, right_dim)
        + dot(tables[at], low, right_dim)
    )


def step_kernel(
    rows_in, cols_in, spectrum, images, wide_in, cols_inv_in, twist_cols_in, twist_rows_in, out,
    led_rows, led_cols, spec, img, wide, cols_inv, twist_cols, twist_rows, grad, update,
    send1, recv1, send2, recv2, send3, recv3, send5, recv5,
    in_sem, known, sent, got,
):
    slab, led = lax.axis_index("slab"), lax.axis_index("led")
    core = lax.rem(slab, NC)
    z = lax.rem(lax.div(slab, NC), NZ)
    y = lax.div(slab, NC * NZ)
    yc = y * NC + core
    idle_y = jnp.where(z < NZ // 2, 0, NY - 1)
    idle = y == idle_y

    def slab_of(ny, nz, nc):
        return (ny * NZ + nz) * NC + nc

    near = [(2, 1), (2, 0), (1, 1), (3, 1), (1, 0), (3, 0), (0, 1)]
    near = [(lax.rem(y + dy, NY), lax.rem(core + dc, NC)) for dy, dc in near]
    far = [lax.rem(z + dz, NZ) for dz in FAR_FIRST]
    across = [lax.rem(led + dx, NX) for dx in (2, 1, 3)]

    loads = [
        pltpu.make_async_copy(a, b, in_sem.at[n])
        for n, (a, b) in enumerate(
            [
                (spectrum, spec),
                (rows_in, led_rows),
                (cols_in, led_cols),
                (twist_cols_in, twist_cols),
                (wide_in.at[0:2], wide.at[0:2]),
                (images, img),
                (twist_rows_in, twist_rows),
                (wide_in.at[2:10], wide.at[2:10]),
                (cols_inv_in, cols_inv),
            ]
        )
    ]
    barrier = pltpu.get_barrier_semaphore()

    links = [lax.rem(z + dz, NZ) for d in LINKS for dz in (d, NZ - d)]

    def greet_links(semaphore):
        for nz in links:
            pl.semaphore_signal(
                semaphore, inc=1, device_id=(slab_of(y, nz, core), led), device_id_type=MESH
            )

    greet_links(barrier)
    for ny, nc in near:
        pl.semaphore_signal(
            barrier, inc=1, device_id=(slab_of(ny, z, nc), led), device_id_type=MESH
        )
    for nx in across:
        pl.semaphore_signal(barrier, inc=1, device_id=(slab, nx), device_id_type=MESH)
    for load in loads:
        load.start()

    row_at = slab * 16 + lax.broadcasted_iota(jnp.int32, (16, 128), 0)
    lane = lax.broadcasted_iota(jnp.int32, (16, 128), 1)

    def term(offset):
        return (2 * offset + 1 - WIN) * (2 * offset + 1 - WIN)

    def inside(l, block):
        return row_terms[l] + term(lane + (block * 128 - led_cols[l])) < WIN * WIN

    def exchange(n_peers, source_of, target_of, peer_of, at):
        for n in range(n_peers):
            pltpu.make_async_remote_copy(
                src_ref=source_of(n),
                dst_ref=target_of(n),
                send_sem=sent.at[at],
                recv_sem=got.at[at],
                device_id=peer_of(n),
                device_id_type=MESH,
            ).start()

    def near_peer(n):
        ny, nc = near[n]
        return slab_of(ny, z, nc), led

    def far_peer(n):
        return slab_of(y, far[n], core), led

    def finish(semaphores, at, block):
        pltpu.make_async_copy(block, block, semaphores.at[at]).wait()

    with jax.named_scope("wait_load"):
        for load in loads[:5]:
            load.wait()
    row_terms = [term(row_at - led_rows[l]) for l in range(2)]
    pieces = []
    for l in range(2):
        values = []
        masks = [inside(l, block) for block in range(16)]
        for n1 in range(8):
            parts = []
            for part in range(2):
                first = spec[part, :, n1 * 128 : n1 * 128 + 128]
                second = spec[part, :, 1024 + n1 * 128 : 1152 + n1 * 128]
                parts.append(
                    jnp.where(masks[n1], first, 0.0) + jnp.where(masks[n1 + 8], second, 0.0)
                )
            values.append(tuple(parts))
        for k1, (re, im) in enumerate(fft(values, -1)):
            a, b = twist_cols[0, k1 : k1 + 1, :], twist_cols[1, k1 : k1 + 1, :]
            pieces.append(jnp.concatenate([re * a + im * b, im * a - re * b], axis=1))
    result = dot_left(wide, COLS_FWD, jnp.concatenate(pieces, axis=0), 1).astype(BF16)
    for l in range(2):
        send1[:, l] = result[:, l * 128 : l * 128 + 128].reshape(8, NZ, 2, 128)
    recv1[yc] = send1[yc]
    for nc in range(NC):
        recv1[idle_y * NC + nc] = jnp.zeros_like(recv1[0])

    @pl.when(idle)
    def _():
        recv3[...] = jnp.zeros_like(recv3)

    with jax.named_scope("wait_barrier"):
        pl.semaphore_wait(barrier, len(links) + len(near) + len(across))
    greet_links(known)

    @pl.when(jnp.logical_not(idle))
    def _():
        exchange(
            len(near),
            lambda n: send1.at[near[n][0] * NC + near[n][1]],
            lambda n: recv1.at[yc],
            near_peer,
            0,
        )

    for load in loads[5:]:
        load.wait()
    moduli = []
    for l in range(2):
        stacked = jnp.concatenate(
            [img[l, :, q * 64 : q * 64 + 64] for q in range(16)], axis=0
        )
        moduli.append(jnp.sqrt(stacked).T)
    moduli = jnp.concatenate(moduli, axis=0)
    tw_re, tw_im = twist_rows[0], twist_rows[1]

    with jax.named_scope("wait_1"):

        @pl.when(jnp.logical_not(idle))
        def _():
            finish(got, 0, recv1.at[0:5])

        @pl.when(idle)
        def _():
            finish(got, 0, recv1.at[0:6])

    send2[...] = recv1[0:4] + recv1[4:8]
    recv2[:, :, z] = send2[:, :, z]
    with jax.named_scope("wait_known"):
        pl.semaphore_wait(known, len(links))
    exchange(
        len(far), lambda n: send2.at[:, :, far[n]], lambda n: recv2.at[:, :, z], far_peer, 1
    )

    with jax.named_scope("wait_2"):
        finish(got, 1, recv2.at[:, :, 0:15])
    strips = recv2[...].reshape(256, 128)
    mixed = dot(wide[ROWS_FWD], strips) + dot(wide[ROWS_FWD + 1], strips)
    rows = []
    for l in range(2):
        re, im = mixed[l * 128 : l * 128 + 64], mixed[l * 128 + 64 : l * 128 + 128]
        rows.append(
            jnp.concatenate([re * tw_re + im * tw_im, im * tw_re - re * tw_im], axis=1)
        )
    rows = jnp.concatenate(rows, axis=0).astype(BF16)
    field = dot(rows, wide[SHORT_FWD]) + dot(rows, wide[SHORT_FWD + 1])
    field_re, field_im = field[:, :128], field[:, 128:]
    factor = moduli / jnp.sqrt(field_re * field_re + field_im * field_im + 0.25) - 1.0
    change = jnp.concatenate([field_re * factor, field_im * factor], axis=1)
    change = change.astype(BF16)
    back = dot(change, wide[SHORT_INV]) + dot(change, wide[SHORT_INV + 1])
    rows = []
    for l in range(2):
        re, im = back[l * 64 : l * 64 + 64, :128], back[l * 64 : l * 64 + 64, 128:]
        rows.append(re * tw_re - im * tw_im)
        rows.append(im * tw_re + re * tw_im)
    rows = jnp.concatenate(rows, axis=0).astype(BF16)
    result = dot(wide[ROWS_INV], rows) + dot(wide[ROWS_INV + 1], rows)
    send3[...] = result.astype(BF16).reshape(64, 4, 128)

    def send_back(ny, nz, nc):
        pltpu.make_async_remote_copy(
            src_ref=send3.at[(lax.rem(ny, 2) * NZ + nz) * NC + nc],
            dst_ref=recv3.at[slab],
            send_sem=sent.at[2],
            recv_sem=got.at[2],
            device_id=(slab_of(ny, nz, nc), led),
            device_id_type=MESH,
        ).start()

    for dz in FAR_FIRST + (0,):
        nz = lax.rem(z + dz, NZ)
        edge = jnp.where(nz < NZ // 2, NY - 1, 0)
        for nc in (NC - 1 - core, core):
            for ny in (edge, 1, 2):
                if dz == 0 and nc is core:
                    pl.when(y != ny)(functools.partial(send_back, ny, nz, nc))
                else:
                    send_back(ny, nz, nc)

    @pl.when(jnp.logical_not(idle))
    def _():
        recv3[slab] = send3[lax.rem(slab, 64)]

    with jax.named_scope("wait_3"):

        @pl.when(jnp.logical_not(idle))
        def _():
            finish(got, 2, recv3.at[0:127])


    home = recv3[...].reshape(512, 128)
    spread = dot(cols_inv[...], home)
    updates = []
    for l in range(2):
        re = spread[l * 256 : l * 256 + 128].T
        im = spread[l * 256 + 128 : l * 256 + 256].T
        values = []
        for k1 in range(8):
            a, b = twist_cols[0, k1 : k1 + 1, :], twist_cols[1, k1 : k1 + 1, :]
            kr, ki = re[k1 * 16 : k1 * 16 + 16], im[k1 * 16 : k1 * 16 + 16]
            values.append((kr * a - ki * b, ki * a + kr * b))
        updates.append(fft(values, 1))
    for l in range(2):
        for n1 in range(8):
            for part in range(2):
                update[l, part, :, n1 * 128 : n1 * 128 + 128] = updates[l][n1][part]
    share = out.shape[2]

    def share_of(nx):
        start = lax.rem(nx, 2) * share
        for block in range(share // 128):
            lanes = pl.ds(pl.multiple_of(start + block * 128, 128), 128)
            masks = [
                row_terms[l] + term(lane + (nx * share + block * 128 - led_cols[l])) < WIN * WIN
                for l in range(2)
            ]
            for part in range(2):
                yield part, slice(block * 128, block * 128 + 128), jnp.where(
                    masks[0], update[0, part, :, lanes], 0.0
                ) + jnp.where(masks[1], update[1, part, :, lanes], 0.0)

    for n, nx in enumerate(across):
        for part, lanes, value in share_of(nx):
            send5[n, part, :, lanes] = value.astype(BF16)
        pltpu.make_async_remote_copy(
            src_ref=send5.at[n],
            dst_ref=recv5.at[n],
            send_sem=sent.at[3],
            recv_sem=got.at[3],
            device_id=(slab, nx),
            device_id_type=MESH,
        ).start()
    for part, lanes, value in share_of(led):
        grad[part, :, lanes] = value
    total = spec[:, :, pl.ds(pl.multiple_of(led * share, share), share)] + grad[...]
    with jax.named_scope("wait_5"):
        finish(got, 3, recv5)
    for n in range(3):
        total = total + recv5[n].astype(F32)
    out[...] = total
    for at, block in ((1, send2.at[:, :, 0:15]), (3, send5.at[0:3])):
        finish(sent, at, block)

    @pl.when(idle)
    def _():
        finish(sent, 2, recv3.at[0:96])

    @pl.when(jnp.logical_not(idle))
    def _():
        finish(sent, 0, send1.at[0:7])
        finish(sent, 2, recv3.at[0:95])


def body(wide, cols_inv, twist_cols, twist_rows, spectrum, led_rows, led_cols, images):
    columns = spectrum.shape[2]
    share = columns // NX
    return pl.pallas_call(
        step_kernel,
        out_shape=pltpu.VMEM((2, 16, share), F32),
        in_specs=[pl.BlockSpec(memory_space=pl.ANY)] * 8,
        out_specs=pl.BlockSpec(memory_space=pltpu.VMEM),
        scratch_shapes=[
            pltpu.SMEM((2,), jnp.int32),
            pltpu.SMEM((2,), jnp.int32),
            pltpu.VMEM((2, 16, columns), F32),
            pltpu.VMEM((2, 8, WIN), F32),
            pltpu.VMEM(wide.shape, BF16),
            pltpu.VMEM(cols_inv.shape, BF16),
            pltpu.VMEM(twist_cols.shape, F32),
            pltpu.VMEM(twist_rows.shape, F32),
            pltpu.VMEM((2, 16, share), F32),
            pltpu.VMEM((2, 2, 16, WIN), F32),
            pltpu.VMEM((8, 2, NZ, 2, 128), BF16),
            pltpu.VMEM((8, 2, NZ, 2, 128), BF16),
            pltpu.VMEM((4, 2, NZ, 2, 128), BF16),
            pltpu.VMEM((4, 2, NZ, 2, 128), BF16),
            pltpu.VMEM((64, 4, 128), BF16),
            pltpu.VMEM((128, 4, 128), BF16),
            pltpu.VMEM((3, 2, 16, share), BF16),
            pltpu.VMEM((3, 2, 16, share), BF16),
            pltpu.SemaphoreType.DMA((9,)),
            pltpu.SemaphoreType.REGULAR,
            pltpu.SemaphoreType.DMA((4,)),
            pltpu.SemaphoreType.DMA((4,)),
        ],
        compiler_params=pltpu.CompilerParams(collective_id=0, has_side_effects=True),
        name="ptychography_step",
    )(led_rows, led_cols, spectrum, images, wide, cols_inv, twist_cols, twist_rows)


def solution(mesh):
    tables = make_tables()
    placed = (P(None, "slab", None), P("led"), P("led"), P("led", "slab", None))
    mapped = jax.shard_map(
        body,
        mesh=mesh,
        in_specs=(P(),) * 4 + placed,
        out_specs=P(None, "slab", "led"),
        check_vma=False,
    )

    def step(spectrum, led_rows, led_cols, images):
        constants = [jnp.asarray(table) for table in tables]
        return mapped(*constants, spectrum, led_rows, led_cols, images)

    return step
```

```python
import functools

import jax
import jax.numpy as jnp
import numpy as np
from jax import lax
from jax.experimental import pallas as pl
from jax.experimental.pallas import tpu as pltpu
from jax.sharding import PartitionSpec as P

NY, NZ, NC, NX = 4, 16, 2, 4
WIN = 1024
MESH = pl.DeviceIdType.MESH
F32, BF16 = jnp.float32, jnp.bfloat16


def grid_of(*sizes):
    return np.meshgrid(*[np.arange(n) for n in sizes], indexing="ij")


def rotation(angle_index, period, out_part, in_part, sign):
    angle = 2.0 * np.pi * (angle_index % period) / period
    same = np.cos(angle)
    cross = sign * np.sin(angle)
    return np.where(out_part == in_part, same, np.where(out_part == 1, cross, -cross))


def split(table):
    high = np.asarray(table, np.float32).astype(BF16)
    low = (table - high.astype(np.float64)).astype(np.float32).astype(BF16)
    return high, low


def make_tables():
    scale = 1.0 / 32.0
    y, c, po, z, pi, n2 = grid_of(NY, NC, 2, NZ, 2, 128)
    k2 = (y * NZ + z) * NC + c
    cols_fwd = scale * rotation(k2 * n2, 128, po, pi, -1).reshape(256, 256)
    z, l, yb, c, p, y2, c2, l2, p2, z2 = grid_of(NZ, 2, 2, NC, 2, NY, NC, 2, 2, NZ)
    hit = (z == z2) & (l == l2) & (p == p2) & (c == c2) & (y2 % 2 == yb)
    fold = hit.astype(np.float64).reshape(256, 512)
    l, po, p, z, l2, yb, c, pi = grid_of(2, 2, 64, NZ, 2, 2, NC, 2)
    strip = 32 * yb + 2 * z + c
    rows_fwd = (scale * rotation(strip * p, 64, po, pi, -1) * (l == l2)).reshape(256, 256)
    strip, l, po, l2, pi, p = grid_of(64, 2, 2, 2, 2, 64)
    rows_inv = (scale * rotation(strip * p, 64, po, pi, 1) * (l == l2)).reshape(256, 256)
    pi, k1, i, po, q, k1o = grid_of(2, 8, 16, 2, 16, 8)
    short_fwd = (rotation(i * q, 16, po, pi, -1) * (k1 == k1o)).reshape(256, 256)
    pi, q, k1, po, k1o, i = grid_of(2, 16, 8, 2, 8, 16)
    short_inv = (rotation(i * q, 16, po, pi, 1) * (k1 == k1o)).reshape(256, 256)
    l, po, n2, k2, l2, pi = grid_of(2, 2, 128, 128, 2, 2)
    cols_inv = (scale * rotation(k2 * n2, 128, po, pi, 1) * (l == l2)).reshape(512, 512)
    wide = []
    for table in (cols_fwd, short_fwd, short_inv, rows_fwd, rows_inv):
        wide.extend(split(table))
    for table in (fold[:, :256], fold[:, 256:]):
        wide.append(np.asarray(table, np.float32).astype(BF16))
    k1, n2 = grid_of(8, 128)
    angle = 2.0 * np.pi * ((k1 * n2) % WIN) / WIN
    twist_cols = np.stack([np.cos(angle), np.sin(angle)]).astype(np.float32)
    p, k1, i = grid_of(64, 8, 16)
    angle = (2.0 * np.pi * ((p * i) % WIN) / WIN).reshape(64, 128)
    twist_rows = np.stack([np.cos(angle), np.sin(angle)]).astype(np.float32)
    return np.stack(wide), split(cols_inv)[0], twist_cols, twist_rows


COLS_FWD, SHORT_FWD, SHORT_INV, ROWS_FWD, ROWS_INV, FOLD = range(0, 12, 2)
LINKS = (1, 3, 4)
FAR_FIRST = (8, 7, 9, 6, 10, 5, 11, 4, 12, 3, 13, 2, 14, 1, 15)


def fft(values, sign):
    size = len(values)
    if size == 1:
        return values
    even, odd = fft(values[0::2], sign), fft(values[1::2], sign)
    low, high = [], []
    for k in range(size // 2):
        (er, ei), (re, im) = even[k], odd[k]
        if k == 0:
            tr, ti = re, im
        elif 4 * k == size:
            tr, ti = (-im, re) if sign > 0 else (im, -re)
        else:
            a = float(np.cos(2 * np.pi * k / size))
            b = float(np.sin(2 * np.pi * k / size)) * sign
            tr, ti = a * re - b * im, a * im + b * re
        low.append((er + tr, ei + ti))
        high.append((er - tr, ei - ti))
    return low + high


def halves(value):
    high = value.astype(BF16)
    return high, (value - high.astype(F32)).astype(BF16)


def dot(left, right, right_dim=0):
    return lax.dot_general(
        left, right, (((1,), (right_dim,)), ((), ())), preferred_element_type=F32
    )


def dot_left(tables, at, value, right_dim=0):
    high, low = halves(value)
    return (
        dot(tables[at], high, right_dim)
        + dot(tables[at + 1], high, right_dim)
        + dot(tables[at], low, right_dim)
    )


def step_kernel(
    rows_in, cols_in, spectrum, images, wide_in, cols_inv_in, twist_cols_in, twist_rows_in, out,
    led_rows, led_cols, spec, img, wide, cols_inv, twist_cols, twist_rows, grad, update,
    send1, recv1, send2, recv2, send3, recv3, send5, recv5,
    in_sem, known, sent, got,
):
    slab, led = lax.axis_index("slab"), lax.axis_index("led")
    core = lax.rem(slab, NC)
    z = lax.rem(lax.div(slab, NC), NZ)
    y = lax.div(slab, NC * NZ)
    yc = y * NC + core
    idle_y = jnp.where(z < NZ // 2, 0, NY - 1)
    idle = y == idle_y

    def slab_of(ny, nz, nc):
        return (ny * NZ + nz) * NC + nc

    near = [(2, 1), (2, 0), (1, 1), (3, 1), (1, 0), (3, 0), (0, 1)]
    near = [(lax.rem(y + dy, NY), lax.rem(core + dc, NC)) for dy, dc in near]
    far = [lax.rem(z + dz, NZ) for dz in FAR_FIRST]
    across = [lax.rem(led + dx, NX) for dx in (2, 1, 3)]

    loads = [
        pltpu.make_async_copy(a, b, in_sem.at[n])
        for n, (a, b) in enumerate(
            [
                (spectrum, spec),
                (rows_in, led_rows),
                (cols_in, led_cols),
                (twist_cols_in, twist_cols),
                (wide_in.at[0:2], wide.at[0:2]),
                (images, img),
                (twist_rows_in, twist_rows),
                (wide_in.at[2:12], wide.at[2:12]),
                (cols_inv_in, cols_inv),
            ]
        )
    ]
    barrier = pltpu.get_barrier_semaphore()

    links = [lax.rem(z + dz, NZ) for d in LINKS for dz in (d, NZ - d)]

    def greet_links(semaphore):
        for nz in links:
            pl.semaphore_signal(
                semaphore, inc=1, device_id=(slab_of(y, nz, core), led), device_id_type=MESH
            )

    greet_links(barrier)
    for ny, nc in near:
        pl.semaphore_signal(
            barrier, inc=1, device_id=(slab_of(ny, z, nc), led), device_id_type=MESH
        )
    for nx in across:
        pl.semaphore_signal(barrier, inc=1, device_id=(slab, nx), device_id_type=MESH)
    for load in loads:
        load.start()

    row_at = slab * 16 + lax.broadcasted_iota(jnp.int32, (16, 128), 0)
    lane = lax.broadcasted_iota(jnp.int32, (16, 128), 1)

    def term(offset):
        return (2 * offset + 1 - WIN) * (2 * offset + 1 - WIN)

    def inside(l, block):
        return row_terms[l] + term(lane + (block * 128 - led_cols[l])) < WIN * WIN

    def exchange(n_peers, source_of, target_of, peer_of, at):
        for n in range(n_peers):
            pltpu.make_async_remote_copy(
                src_ref=source_of(n),
                dst_ref=target_of(n),
                send_sem=sent.at[at],
                recv_sem=got.at[at],
                device_id=peer_of(n),
                device_id_type=MESH,
            ).start()

    def near_peer(n):
        ny, nc = near[n]
        return slab_of(ny, z, nc), led

    def far_peer(n):
        return slab_of(y, far[n], core), led

    def finish(semaphores, at, block):
        pltpu.make_async_copy(block, block, semaphores.at[at]).wait()

    with jax.named_scope("wait_load"):
        for load in loads[:5]:
            load.wait()
    row_terms = [term(row_at - led_rows[l]) for l in range(2)]
    pieces = []
    for l in range(2):
        values = []
        masks = [inside(l, block) for block in range(16)]
        for n1 in range(8):
            parts = []
            for part in range(2):
                first = spec[part, :, n1 * 128 : n1 * 128 + 128]
                second = spec[part, :, 1024 + n1 * 128 : 1152 + n1 * 128]
                parts.append(
                    jnp.where(masks[n1], first, 0.0) + jnp.where(masks[n1 + 8], second, 0.0)
                )
            values.append(tuple(parts))
        for k1, (re, im) in enumerate(fft(values, -1)):
            a, b = twist_cols[0, k1 : k1 + 1, :], twist_cols[1, k1 : k1 + 1, :]
            pieces.append(jnp.concatenate([re * a + im * b, im * a - re * b], axis=1))
    result = dot_left(wide, COLS_FWD, jnp.concatenate(pieces, axis=0), 1).astype(BF16)
    for l in range(2):
        send1[:, l * 32 : l * 32 + 32] = result[:, l * 128 : l * 128 + 128].reshape(8, 32, 128)
    recv1[yc] = send1[yc]
    for nc in range(NC):
        recv1[idle_y * NC + nc] = jnp.zeros_like(recv1[0])

    @pl.when(idle)
    def _():
        recv3[...] = jnp.zeros_like(recv3)

    with jax.named_scope("wait_barrier"):
        pl.semaphore_wait(barrier, len(links) + len(near) + len(across))
    greet_links(known)

    @pl.when(jnp.logical_not(idle))
    def _():
        exchange(
            len(near),
            lambda n: send1.at[near[n][0] * NC + near[n][1]],
            lambda n: recv1.at[yc],
            near_peer,
            0,
        )

    for load in loads[5:]:
        load.wait()
    moduli = []
    for l in range(2):
        stacked = jnp.concatenate(
            [img[l, :, q * 64 : q * 64 + 64] for q in range(16)], axis=0
        )
        moduli.append(jnp.sqrt(stacked).T)
    moduli = jnp.concatenate(moduli, axis=0)
    tw_re, tw_im = twist_rows[0], twist_rows[1]

    with jax.named_scope("wait_1"):

        @pl.when(jnp.logical_not(idle))
        def _():
            finish(got, 0, recv1.at[0:5])

        @pl.when(idle)
        def _():
            finish(got, 0, recv1.at[0:6])

    moved = dot(wide[FOLD], recv1[0:4].reshape(256, 128)) + dot(
        wide[FOLD + 1], recv1[4:8].reshape(256, 128)
    )
    send2[...] = moved.astype(BF16).reshape(16, 16, 128)
    recv2[z] = send2[z]
    with jax.named_scope("wait_known"):
        pl.semaphore_wait(known, len(links))
    exchange(
        len(far), lambda n: send2.at[far[n]], lambda n: recv2.at[z], far_peer, 1
    )

    with jax.named_scope("wait_2"):
        finish(got, 1, recv2.at[0:15])
    strips = recv2[...].reshape(256, 128)
    mixed = dot(wide[ROWS_FWD], strips) + dot(wide[ROWS_FWD + 1], strips)
    rows = []
    for l in range(2):
        re, im = mixed[l * 128 : l * 128 + 64], mixed[l * 128 + 64 : l * 128 + 128]
        rows.append(
            jnp.concatenate([re * tw_re + im * tw_im, im * tw_re - re * tw_im], axis=1)
        )
    rows = jnp.concatenate(rows, axis=0).astype(BF16)
    field = dot(rows, wide[SHORT_FWD]) + dot(rows, wide[SHORT_FWD + 1])
    field_re, field_im = field[:, :128], field[:, 128:]
    factor = moduli / jnp.sqrt(field_re * field_re + field_im * field_im + 0.25) - 1.0
    change = jnp.concatenate([field_re * factor, field_im * factor], axis=1)
    change = change.astype(BF16)
    back = dot(change, wide[SHORT_INV]) + dot(change, wide[SHORT_INV + 1])
    rows = []
    for l in range(2):
        re, im = back[l * 64 : l * 64 + 64, :128], back[l * 64 : l * 64 + 64, 128:]
        rows.append(re * tw_re - im * tw_im)
        rows.append(im * tw_re + re * tw_im)
    rows = jnp.concatenate(rows, axis=0).astype(BF16)
    result = dot(wide[ROWS_INV], rows) + dot(wide[ROWS_INV + 1], rows)
    send3[...] = result.astype(BF16).reshape(64, 4, 128)

    def send_back(ny, nz, nc):
        pltpu.make_async_remote_copy(
            src_ref=send3.at[(lax.rem(ny, 2) * NZ + nz) * NC + nc],
            dst_ref=recv3.at[slab],
            send_sem=sent.at[2],
            recv_sem=got.at[2],
            device_id=(slab_of(ny, nz, nc), led),
            device_id_type=MESH,
        ).start()

    for dz in FAR_FIRST + (0,):
        nz = lax.rem(z + dz, NZ)
        edge = jnp.where(nz < NZ // 2, NY - 1, 0)
        for nc in (NC - 1 - core, core):
            for ny in (edge, 1, 2):
                if dz == 0 and nc is core:
                    pl.when(y != ny)(functools.partial(send_back, ny, nz, nc))
                else:
                    send_back(ny, nz, nc)

    @pl.when(jnp.logical_not(idle))
    def _():
        recv3[slab] = send3[lax.rem(slab, 64)]

    with jax.named_scope("wait_3"):

        @pl.when(jnp.logical_not(idle))
        def _():
            finish(got, 2, recv3.at[0:127])


    home = recv3[...].reshape(512, 128)
    spread = dot(cols_inv[...], home)
    updates = []
    for l in range(2):
        re = spread[l * 256 : l * 256 + 128].T
        im = spread[l * 256 + 128 : l * 256 + 256].T
        values = []
        for k1 in range(8):
            a, b = twist_cols[0, k1 : k1 + 1, :], twist_cols[1, k1 : k1 + 1, :]
            kr, ki = re[k1 * 16 : k1 * 16 + 16], im[k1 * 16 : k1 * 16 + 16]
            values.append((kr * a - ki * b, ki * a + kr * b))
        updates.append(fft(values, 1))
    for l in range(2):
        for n1 in range(8):
            for part in range(2):
                update[l, part, :, n1 * 128 : n1 * 128 + 128] = updates[l][n1][part]
    share = out.shape[2]

    def share_of(nx):
        start = lax.rem(nx, 2) * share
        for block in range(share // 128):
            lanes = pl.ds(pl.multiple_of(start + block * 128, 128), 128)
            masks = [
                row_terms[l] + term(lane + (nx * share + block * 128 - led_cols[l])) < WIN * WIN
                for l in range(2)
            ]
            for part in range(2):
                yield part, slice(block * 128, block * 128 + 128), jnp.where(
                    masks[0], update[0, part, :, lanes], 0.0
                ) + jnp.where(masks[1], update[1, part, :, lanes], 0.0)

    for n, nx in enumerate(across):
        for part, lanes, value in share_of(nx):
            send5[n, part, :, lanes] = value.astype(BF16)
        pltpu.make_async_remote_copy(
            src_ref=send5.at[n],
            dst_ref=recv5.at[n],
            send_sem=sent.at[3],
            recv_sem=got.at[3],
            device_id=(slab, nx),
            device_id_type=MESH,
        ).start()
    for part, lanes, value in share_of(led):
        grad[part, :, lanes] = value
    total = spec[:, :, pl.ds(pl.multiple_of(led * share, share), share)] + grad[...]
    with jax.named_scope("wait_5"):
        finish(got, 3, recv5)
    for n in range(3):
        total = total + recv5[n].astype(F32)
    out[...] = total
    for at, block in ((1, send2.at[0:15]), (3, send5.at[0:3])):
        finish(sent, at, block)

    @pl.when(idle)
    def _():
        finish(sent, 2, recv3.at[0:96])

    @pl.when(jnp.logical_not(idle))
    def _():
        finish(sent, 0, send1.at[0:7])
        finish(sent, 2, recv3.at[0:95])


def body(wide, cols_inv, twist_cols, twist_rows, spectrum, led_rows, led_cols, images):
    columns = spectrum.shape[2]
    share = columns // NX
    return pl.pallas_call(
        step_kernel,
        out_shape=pltpu.VMEM((2, 16, share), F32),
        in_specs=[pl.BlockSpec(memory_space=pl.ANY)] * 8,
        out_specs=pl.BlockSpec(memory_space=pltpu.VMEM),
        scratch_shapes=[
            pltpu.SMEM((2,), jnp.int32),
            pltpu.SMEM((2,), jnp.int32),
            pltpu.VMEM((2, 16, columns), F32),
            pltpu.VMEM((2, 8, WIN), F32),
            pltpu.VMEM(wide.shape, BF16),
            pltpu.VMEM(cols_inv.shape, BF16),
            pltpu.VMEM(twist_cols.shape, F32),
            pltpu.VMEM(twist_rows.shape, F32),
            pltpu.VMEM((2, 16, share), F32),
            pltpu.VMEM((2, 2, 16, WIN), F32),
            pltpu.VMEM((8, 64, 128), BF16),
            pltpu.VMEM((8, 64, 128), BF16),
            pltpu.VMEM((16, 16, 128), BF16),
            pltpu.VMEM((16, 16, 128), BF16),
            pltpu.VMEM((64, 4, 128), BF16),
            pltpu.VMEM((128, 4, 128), BF16),
            pltpu.VMEM((3, 2, 16, share), BF16),
            pltpu.VMEM((3, 2, 16, share), BF16),
            pltpu.SemaphoreType.DMA((9,)),
            pltpu.SemaphoreType.REGULAR,
            pltpu.SemaphoreType.DMA((4,)),
            pltpu.SemaphoreType.DMA((4,)),
        ],
        compiler_params=pltpu.CompilerParams(collective_id=0, has_side_effects=True),
        name="ptychography_step",
    )(led_rows, led_cols, spectrum, images, wide, cols_inv, twist_cols, twist_rows)


def solution(mesh):
    tables = make_tables()
    placed = (P(None, "slab", None), P("led"), P("led"), P("led", "slab", None))
    mapped = jax.shard_map(
        body,
        mesh=mesh,
        in_specs=(P(),) * 4 + placed,
        out_specs=P(None, "slab", "led"),
        check_vma=False,
    )

    def step(spectrum, led_rows, led_cols, images):
        constants = [jnp.asarray(table) for table in tables]
        return mapped(*constants, spectrum, led_rows, led_cols, images)

    return step
```
